32 devices in a mesh: groups: 2 (over y), tile: 4 (over z), chan: 2 (over x), sub: 2 (over core).
Axes of the slice: x: 2, y: 2, z: 4, core: 2. Of those that a mesh axis runs over, the one named last changes fastest.
Arguments:
- cycle_maps: bfloat16 [8, 3, 65536], P(('groups', 'chan', 'sub'), None, 'tile'), parts along dimension 0, may hold values from -6 to 6
- send_pick: int32 [98304], P('tile'), may hold values from 0 to 16384, as said below
- recv_pick: int32 [65536], P('tile'), may hold values from 0 to 24575, as said below
- neighbour: int32 [4, 4], replicated, may hold values from -1 to 3, as said below
- facing: int32 [4, 4], replicated, may hold values from 0 to 3, as said below
- conv_first: bfloat16 [9, 64, 3], replicated, may hold values from -1.25 to 1.25
- conv_second: bfloat16 [9, 64, 64], replicated, may hold values from -0.25 to 0.25
- cotangent: bfloat16 [8, 64, 65536], P(('groups', 'chan', 'sub'), None, 'tile'), parts along dimension 0, may hold values from -6 to 6
Outputs:
- output_maps: bfloat16 [8, 64, 65536], P(('groups', 'chan', 'sub'), None, 'tile'), parts along dimension 0
- grad_hidden: bfloat16 [8, 64, 65536], P(('groups', 'chan', 'sub'), None, 'tile'), parts along dimension 0
- grad_first: float32 [18, 64, 3], P('groups'), parts along dimension 0
- grad_second: float32 [18, 64, 64], P('groups'), parts along dimension 0
The draws below stay inside these ranges and needn't reach their ends.
There are 2 independent parts, one for each index of `groups`. The reference program is written for one: setup_inputs(seed, part) draws one part's arguments, and reference() takes and returns one part's arrays. A program takes and returns all parts, laid end to end along the dimension named above; an argument that names none is the same for every part. Nothing has to cross between parts.
Inputs may be any that keep to these rules, and one draw needn't show every extreme that they name: `send_pick`: entry ((i * 4) + d) * 6144 + s names the cycle pixel (0 to 16383, local to owner i) that owner i puts into slot s of its block for tile d, or 16384 for an empty slot; the used slots of each block are 0 to n - 1 with n at most 6144, and some block is full. Every cycle pixel is named exactly once. `recv_pick`: entry d * 16384 + q is i * 6144 + s: pixel q of tile d is carried in slot s of owner i's block for tile d, a used slot. With send_pick it maps cycle pixels one to one onto tile pixels; each tile receives from every owner. `neighbour`: the tiles form a band four tiles tall, closed east to west; each tile is turned by a multiple of a right angle. Row t lists the tile across sides north, east, south, west of tile t in its own orientation, -1 beyond the band's rim. Adjacency is mutual: if side k of t touches side j of p, side j of p touches side k of t. A tile meets one tile on at most 2 sides, and some tile on exactly that many. `facing`: the side of the neighbouring tile that touches side k of tile t; 0 where there is no neighbour.
All inputs are finite; a program needn't handle non-finite values.
Results may differ from the reference program's by a relative error of at most 0.005.
Values may be sent and summed in bfloat16 or wider, within the bound.
No kernel may reach another device: no remote copies, remote signals or barrier semaphores. Data moves between devices by JAX's collectives and lax.ppermute only.
A program may use at most 192 MiB of HBM per device.

```python
import math
import jax
import jax.numpy as jnp
from jax import lax

SIDE = 128
CH = 64
CIN = 3
TILES = 4
CAP = 6144
BATCH = 4
NPIX = 65536
N_TILE = 4


def draw_order(order_key):
    return jax.random.permutation(order_key, SIDE * SIDE).astype(jnp.int32)


def regroup_tables(key):
    tile_count = N_TILE
    pixel_count = SIDE * SIDE
    pair_total = 2 * pixel_count // tile_count
    spread_half = pair_total // 4
    count_key, order_key = jax.random.split(jax.random.fold_in(key, 11))
    couples = tile_count // 4
    base = jax.random.randint(count_key, (couples, tile_count), pair_total // 2 - spread_half, pair_total // 2 + spread_half + 1).astype(jnp.int32)
    base = base.at[0, 0].set(pair_total // 2 + spread_half)
    paired = jnp.stack([base, pair_total - base], axis=1).reshape(2 * couples, tile_count)
    first_part = paired.T
    second_part = pair_total - jnp.roll(paired, -1, axis=1).T
    counts = jnp.stack([first_part, second_part], axis=2).reshape(tile_count, tile_count)
    sources = jnp.arange(tile_count, dtype=jnp.int32)
    shifts = (sources[None, :] - sources[:, None]) % tile_count
    by_dest = jnp.take_along_axis(counts, shifts, axis=1)
    starts = jnp.cumsum(counts, axis=1) - counts
    start_dest = jnp.take_along_axis(starts, shifts, axis=1)
    slot_ids = jnp.arange(CAP, dtype=jnp.int32)
    send_table = jnp.where(slot_ids[None, None, :] < by_dest[:, :, None], start_dest[:, :, None] + slot_ids[None, None, :], pixel_count)
    column_end = jnp.cumsum(by_dest, axis=0)
    column_start = column_end - by_dest
    positions = jnp.arange(pixel_count, dtype=jnp.int32)
    source_of = jnp.sum((positions[None, :, None] >= column_end.T[:, None, :]).astype(jnp.int32), axis=2)
    start_of = jnp.take_along_axis(column_start.T, source_of, axis=1)
    values = source_of * CAP + positions[None, :] - start_of
    orders = jax.vmap(draw_order)(jax.random.split(order_key, tile_count))
    recv_table = jnp.zeros((tile_count, pixel_count), jnp.int32).at[sources[:, None], orders].set(values.astype(jnp.int32))
    return (send_table.reshape(-1).astype(jnp.int32), recv_table.reshape(-1))


def face_tables(key):
    tile_count = N_TILE
    columns = tile_count // 4
    place_key, turn_key = jax.random.split(jax.random.fold_in(key, 23))
    place = jax.random.permutation(place_key, tile_count).astype(jnp.int32)
    turn = jax.random.randint(turn_key, (tile_count,), 0, 4).astype(jnp.int32)
    owner = jnp.zeros((tile_count,), jnp.int32).at[place].set(jnp.arange(tile_count, dtype=jnp.int32))
    grid_row = place // columns
    grid_col = place % columns
    row_step = jnp.array([-1, 0, 1, 0], jnp.int32)
    col_step = jnp.array([0, 1, 0, -1], jnp.int32)
    heading = (jnp.arange(4, dtype=jnp.int32)[None, :] + turn[:, None]) % 4
    next_row = grid_row[:, None] + row_step[heading]
    next_col = (grid_col[:, None] + col_step[heading]) % columns
    inside = (next_row >= 0) & (next_row < 4)
    partner = owner[jnp.clip(next_row, 0, 3) * columns + next_col]
    neighbour = jnp.where(inside, partner, -1).astype(jnp.int32)
    facing = jnp.where(inside, (heading + 2 - turn[partner]) % 4, 0).astype(jnp.int32)
    return (neighbour, facing)


def draw_send_pick(key, part):
    return regroup_tables(key)[0]


def draw_recv_pick(key, part):
    return regroup_tables(key)[1]


def draw_neighbour(key, part):
    return face_tables(key)[0]


def draw_facing(key, part):
    return face_tables(key)[1]


def block_scale(own_key, extent, pieces, least, largest):
    def one(dim, parts):
        draws = jax.random.uniform(jax.random.fold_in(jax.random.fold_in(own_key, 6), dim), (parts,), jnp.float32, least / len(pieces), largest / len(pieces))
        return jnp.repeat(jnp.exp(draws), extent[dim] // parts).reshape((-1,) + (1,) * (len(extent) - dim - 1))

    loudness = one(*pieces[0])
    for cut in pieces[1:]:
        loudness = loudness * one(*cut)
    return loudness


def bell_draw(key, dims, scale, bound, cuts=(), kind=jnp.bfloat16):
    factor_of = block_scale(key, dims, cuts, -0.22, 0.18) if cuts else 1.0
    values = jax.random.normal(key, dims, jnp.float32) * scale * factor_of
    return jnp.minimum(jnp.maximum(values, -bound), bound).astype(kind)


def setup_inputs(seed: int = 0, part: int = 0) -> dict:
    splits = jax.random.split(jax.random.key(seed), 9)
    own_keys = jax.random.split(jax.random.fold_in(splits[8], part), 9)
    cycle_maps = bell_draw(own_keys[0], (BATCH, CIN, NPIX), 1.0, 6.0, ((0, 4), (2, 4)))
    send_pick = draw_send_pick(jax.random.fold_in(splits[8], 71), part)
    recv_pick = draw_recv_pick(jax.random.fold_in(splits[8], 71), part)
    neighbour = draw_neighbour(jax.random.fold_in(splits[8], 71), part)
    facing = draw_facing(jax.random.fold_in(splits[8], 71), part)
    conv_first = bell_draw(splits[5], (9, CH, CIN), (9 * CIN) ** -0.5, 1.25)
    conv_second = bell_draw(splits[6], (9, CH, CH), (9 * CH) ** -0.5, 0.25)
    cotangent = bell_draw(own_keys[7], (BATCH, CH, NPIX), 1.0, 6.0, ((0, 4), (2, 4)))
    return dict(cycle_maps=cycle_maps, send_pick=send_pick, recv_pick=recv_pick, neighbour=neighbour, facing=facing, conv_first=conv_first, conv_second=conv_second, cotangent=cotangent)


def border(field):
    return jnp.stack([field[:, :, 0, :], field[:, :, :, -1], field[:, :, -1, :], field[:, :, :, 0]])

def frame_rim(frame):
    return jnp.stack([frame[:, :, 0, 1:-1], frame[:, :, 1:-1, -1], frame[:, :, -1, 1:-1], frame[:, :, 1:-1, 0]])

def outgoing(strips):
    return jnp.stack([strips[0], strips[1], strips[2][..., ::-1], strips[3][..., ::-1]])

def orient(strips):
    return jnp.stack([strips[0][..., ::-1], strips[1][..., ::-1], strips[2], strips[3]])

def route(strips, neighbour, facing):
    partner = jnp.maximum(neighbour, 0)
    arrived = strips[facing, partner]
    arrived = jnp.where((neighbour >= 0)[:, :, None, None], arrived, jnp.zeros((), strips.dtype))
    return orient(jnp.transpose(arrived, (1, 0, 2, 3)))

def with_rims(field, incoming):
    padded = jnp.pad(field, ((0, 0), (0, 0), (1, 1), (1, 1)))
    padded = padded.at[:, :, 0, 1:-1].set(incoming[0])
    padded = padded.at[:, :, 1:-1, -1].set(incoming[1])
    padded = padded.at[:, :, -1, 1:-1].set(incoming[2])
    padded = padded.at[:, :, 1:-1, 0].set(incoming[3])
    return padded

def convolve(padded, weights):
    total = None
    for position in range(9):
        row_shift, col_shift = divmod(position, 3)
        window = padded[:, :, row_shift:row_shift + SIDE, col_shift:col_shift + SIDE].astype(jnp.float32)
        term = jnp.einsum('oc,tcij->toij', weights[position], window)
        total = term if total is None else total + term
    return total

def weight_terms(padded, grad_out):
    terms = []
    for position in range(9):
        row_shift, col_shift = divmod(position, 3)
        window = padded[:, :, row_shift:row_shift + SIDE, col_shift:col_shift + SIDE].astype(jnp.float32)
        terms.append(jnp.einsum('toij,tcij->oc', grad_out, window))
    return jnp.stack(terms)

def spread(grad_out, weights):
    total = None
    for position in range(9):
        row_shift, col_shift = divmod(position, 3)
        term = jnp.einsum('oc,toij->tcij', weights[position], grad_out)
        term = jnp.pad(term, ((0, 0), (0, 0), (row_shift, 2 - row_shift), (col_shift, 2 - col_shift)))
        total = term if total is None else total + term
    return total

def add_rims(interior, incoming):
    interior = interior.at[:, :, 0, :].add(incoming[0])
    interior = interior.at[:, :, :, -1].add(incoming[1])
    interior = interior.at[:, :, -1, :].add(incoming[2])
    interior = interior.at[:, :, :, 0].add(incoming[3])
    return interior

def reference(cycle_maps, send_pick, recv_pick, neighbour, facing, conv_first, conv_second, cotangent):
    pixel_count = SIDE * SIDE
    tile_pixel = jnp.arange(NPIX, dtype=jnp.int32)
    dest_tile = tile_pixel // pixel_count
    source = recv_pick // CAP
    slot_index = recv_pick % CAP
    local = send_pick[source * (TILES * CAP) + dest_tile * CAP + slot_index]
    cycle_index = (source * pixel_count + local).astype(jnp.int32)
    first_f = conv_first.astype(jnp.float32)
    second_f = conv_second.astype(jnp.float32)
    scale = 1.0 / math.sqrt(BATCH * NPIX)

    def one_map(carry, inputs):
        cycle, grad_in = inputs
        tiles = jnp.transpose(cycle[:, cycle_index].reshape(CIN, TILES, SIDE, SIDE), (1, 0, 2, 3))
        padded_in = with_rims(tiles, route(outgoing(border(tiles)), neighbour, facing))
        pre = convolve(padded_in, first_f)
        hidden = jax.nn.silu(pre).astype(jnp.bfloat16)
        padded_hidden = with_rims(hidden, route(outgoing(border(hidden)), neighbour, facing))
        output = convolve(padded_hidden, second_f).astype(jnp.bfloat16)
        grad_out = jnp.transpose(grad_in.reshape(CH, TILES, SIDE, SIDE), (1, 0, 2, 3)).astype(jnp.float32)
        second_term = weight_terms(padded_hidden, grad_out)
        grad_frame = spread(grad_out, second_f)
        rim_grads = route(outgoing(frame_rim(grad_frame)).astype(jnp.bfloat16), neighbour, facing)
        hidden_grad = add_rims(grad_frame[:, :, 1:-1, 1:-1], rim_grads.astype(jnp.float32))
        sigma = jax.nn.sigmoid(pre)
        pre_grad = (hidden_grad * sigma * (1.0 + pre * (1.0 - sigma))).astype(jnp.bfloat16)
        first_term = weight_terms(padded_in, pre_grad.astype(jnp.float32))
        out_maps = jnp.transpose(output, (1, 0, 2, 3)).reshape(CH, NPIX)
        out_grad = jnp.transpose(hidden_grad.astype(jnp.bfloat16), (1, 0, 2, 3)).reshape(CH, NPIX)
        return ((carry[0] + first_term, carry[1] + second_term), (out_maps, out_grad))
    start = (jnp.zeros((9, CH, CIN), jnp.float32), jnp.zeros((9, CH, CH), jnp.float32))
    (first_sum, second_sum), (output_maps, grad_hidden) = lax.scan(one_map, start, (cycle_maps, cotangent))
    return (output_maps, grad_hidden, first_sum * scale, second_sum * scale)
```

```python
import functools
import math

import jax
import jax.numpy as jnp
from jax import lax
from jax.experimental import pallas as pl
from jax.experimental.pallas import tpu as pltpu
from jax.sharding import PartitionSpec as P

SIDE = 128
PIX = SIDE * SIDE
CH = 64
CIN = 3
LOW = 256
COMB = 80
ROWS = 16
STEPS = SIDE // ROWS
F32 = jnp.float32
BF16 = jnp.bfloat16
SMEM = pl.BlockSpec(memory_space=pltpu.SMEM)
VMEM = pl.BlockSpec(memory_space=pltpu.VMEM)


def iota(shape, dim):
    return lax.broadcasted_iota(jnp.int32, shape, dim)


def hot(a, b):
    return jnp.where(a == b, 1.0, 0.0).astype(BF16)


def dot(a, b):
    return jnp.dot(a, b, preferred_element_type=F32)


def dot_nt(a, b):
    return lax.dot_general(a, b, (((1,), (1,)), ((), ())), preferred_element_type=F32)


def reverse(strip):
    swap = hot(iota((SIDE, SIDE), 0) + iota((SIDE, SIDE), 1), SIDE - 1)
    return dot(strip.astype(BF16), swap)


def from_left(x):
    return jnp.where(iota(x.shape, 1) == 0, 0.0, pltpu.roll(x, 1, 1))


def from_right(x):
    return jnp.where(iota(x.shape, 1) == SIDE - 1, 0.0, pltpu.roll(x, SIDE - 1, 1))


def ends_table(shift, east):
    src = iota((SIDE, 2 * SIDE), 0)
    lane = iota((SIDE, 2 * SIDE), 1)
    return hot(lane, 2 * (src - shift) + (0 if east else 1))


def row_ends(pairs, row):
    half = row // (SIDE // 2)
    back = lax.rem(4 * SIDE - 2 * row - 1, SIDE)
    return pltpu.roll(pairs[half], back, 1)


def is_end(shape):
    lane = iota(shape, 1)
    return (lane == 0) | (lane == SIDE - 1)


def pick_rows(low_rows, high_rows, groups, source):
    found = dot(source, hot(iota((LOW, LOW), 0), low_rows))
    here = iota((groups, LOW), 0) == high_rows
    picked = []
    for c in range(CIN):
        part = jnp.where(here, found[c * groups : (c + 1) * groups], 0.0)
        picked.append(jnp.sum(part, axis=0, keepdims=True))
    return picked


def split_index(index):
    return index & (LOW - 1), index >> 8


def tile_params(limit_mib):
    return pltpu.CompilerParams(vmem_limit_bytes=limit_mib << 20)


def send_kernel(tile_count, direct, scal, cyc, index, *rest):
    outs, (stage, source, found) = rest[:-3], rest[-3:]
    groups = PIX // LOW
    per_dest = index.shape[0] // 2 // tile_count
    whole = cyc[...].astype(F32)
    for h in range(groups):
        piece = whole[:, h * LOW : (h + 1) * LOW]
        for c in range(CIN):
            stage[pl.ds(c * groups + h, 1), :] = piece[c : c + 1]
    source[...] = stage[...].astype(BF16)
    data = source[...]
    me = scal[0]

    def chunk(m, carry):
        if direct:
            dest = lax.rem(me + m // per_dest, tile_count)
            at = dest * per_dest + lax.rem(m, per_dest)
        else:
            at = m
        row = jnp.concatenate([index[pl.ds(2 * at, 1), :], index[pl.ds(2 * at + 1, 1), :]], axis=1)
        low, high = split_index(row)
        picked = pick_rows(low, high, groups, data)
        for c in range(CIN):
            found[c, pl.ds(m, 1), :] = picked[c]
        return carry

    lax.fori_loop(0, tile_count * per_dest, chunk, 0, unroll=4)
    for d in range(tile_count):
        for c in range(CIN):
            block = found[c, d * per_dest : (d + 1) * per_dest, :].astype(BF16)
            if direct:
                outs[d][c] = block
            else:
                outs[0][d, c] = block


def side_towards(nbr, me, dest):
    side = jnp.int32(0)
    for k in range(4):
        side = jnp.where(nbr[me, k] == dest, k, side)
    return side


def send_strips(tile_count, direct, nbr, me, strips, outs):
    if direct:
        for s in range(1, tile_count):
            dest = lax.rem(me + s, tile_count)
            outs[s - 1][...] = strips[side_towards(nbr, me, dest)]
    else:
        for dest in range(tile_count):
            outs[0][dest] = strips[side_towards(nbr, me, dest)]


def take_strips(tile_count, direct, nbr, fac, me, own, arrived, table):
    for k in range(4):
        table[k] = own[k]
    if direct:
        for s in range(1, tile_count):
            table[4 + lax.rem(me + tile_count - s, tile_count)] = arrived[s - 1][...]
    else:
        for d in range(tile_count):
            table[4 + d] = arrived[0][d]
    table[4 + tile_count] = jnp.zeros(table.shape[1:], table.dtype)
    got = []
    for k in range(4):
        other = nbr[me, k]
        at = jnp.where(other == me, fac[me, k], 4 + other)
        at = jnp.where(other < 0, 4 + tile_count, at)
        got.append(table[at])
    return got


def strip_kernel(tile_count, direct, scal, nbr, index, rims, *rest):
    n_in = tile_count if direct else 1
    n_out = tile_count - 1 if direct else 1
    blocks, rest = rest[:n_in], rest[n_in:]
    sends, rest = rest[:n_out], rest[n_out:]
    source, strips, comb, stage = rest
    me = scal[0]
    per_src = blocks[0].shape[-2]
    groups = tile_count * per_src
    for s in range(tile_count):
        for c in range(CIN):
            if direct:
                src = lax.rem(me + tile_count - s, tile_count)
                at = c * groups + src * per_src
                if per_src % 8 == 0:
                    at = pl.multiple_of(at, 8)
                stage[pl.ds(at, per_src), :] = blocks[s][c].astype(F32)
            else:
                at = c * groups + s * per_src
                stage[at : at + per_src, :] = blocks[0][s, c].astype(F32)
    source[...] = stage[...].astype(BF16)
    data = source[...]
    flipped = index[...].astype(F32).T
    col = lambda j: flipped[j : j + 1, :].astype(jnp.int32)
    row = lambda i: index[i : i + 1, :]
    pairs = [(row(0), row(1)), (row(126), row(127)), (col(0), col(1)), (col(126), col(127))]
    for n, pair in enumerate(pairs):
        low, high = split_index(jnp.concatenate(pair, axis=1))
        picked = pick_rows(low, high, groups, data)
        for c in range(CIN):
            strips[2 * n, c : c + 1, :] = picked[c][:, :SIDE]
            strips[2 * n + 1, c : c + 1, :] = picked[c][:, SIDE:]
    for n in range(8):
        strips[n, CIN:, :] = jnp.zeros((8 - CIN, SIDE), F32)
    edge = [strips[0], strips[7], reverse(strips[3]), reverse(strips[4])]
    blank = jnp.zeros((COMB - CH - 8, SIDE), F32)
    for k in range(4):
        comb[k, :CH, :] = rims[k]
        comb[k, CH:, :] = jnp.concatenate([edge[k], blank], axis=0).astype(BF16)
    send_strips(tile_count, direct, nbr, me, comb, sends)


def main_pick_kernel(groups, index, source, out):
    data = source[...]

    def chunk(m, carry):
        row = jnp.concatenate([index[pl.ds(2 * m, 1), :], index[pl.ds(2 * m + 1, 1), :]], axis=1)
        low, high = split_index(row)
        picked = pick_rows(low, high, groups, data)
        lanes = pl.ds(pl.multiple_of(m * LOW, LOW), LOW)
        for c in range(CIN):
            out[c : c + 1, lanes] = picked[c]
        return carry

    lax.fori_loop(0, PIX // LOW, chunk, 0, unroll=4)
    out[CIN:, :] = jnp.zeros((8 - CIN, PIX), F32)


def three_rows_down(before, here, after):
    up = jnp.concatenate([here[:, SIDE:], after], axis=1)
    down = jnp.concatenate([before, here[:, :-SIDE]], axis=1)
    return jnp.concatenate([up, here, down], axis=0)


def frame_kernel(cot, prev, nxt, conv_second, hg, rims, ends, fwd_w, back_w, columns):
    step = pl.program_id(0)

    @pl.when(step == 0)
    def _():
        for a in range(3):
            for b in range(3):
                w = conv_second[3 * a + b]
                rows = slice(b * CH, (b + 1) * CH)
                lanes = slice(a * CH, (a + 1) * CH)
                fwd_w[rows, lanes] = w
                back_w[rows, lanes] = w.astype(F32).T.astype(BF16)
        columns[...] = jnp.zeros_like(columns)

    weights = back_w[...]
    here = cot[...]
    before = jnp.where(step > 0, prev[...], jnp.zeros_like(prev))
    after = jnp.where(step < STEPS - 1, nxt[...], jnp.zeros_like(nxt))
    stacked = three_rows_down(before, here, after)
    for p in range(ROWS // 2):
        lanes = slice(2 * p * SIDE, (2 * p + 2) * SIDE)
        z = dot(weights, stacked[:, lanes])
        for r in range(2):
            zr = z[:, r * SIDE : (r + 1) * SIDE]
            hg[:, (2 * p + r) * SIDE : (2 * p + r + 1) * SIDE] = (
                zr[CH : 2 * CH] + from_right(zr[:CH]) + from_left(zr[2 * CH :])
            )
    half = step // (STEPS // 2)
    acc = columns[half]
    pair = iota((CH, SIDE), 1) // 2
    for t in range(ROWS):
        r = step * ROWS + t
        line = here[:, t * SIDE : (t + 1) * SIDE].astype(F32)
        turned = pltpu.roll(line, lax.rem(2 * r + 1, SIDE), 1)
        acc = jnp.where(pair == lax.rem(r, SIDE // 2), turned, acc)
    columns[half] = acc

    def rim_row(line, a):
        z = dot(weights[:, a * CH : (a + 1) * CH], line)
        return z[CH : 2 * CH] + from_right(z[:CH]) + from_left(z[2 * CH :])

    @pl.when(step == 0)
    def _():
        rims[0] = rim_row(here[:, :SIDE], 0).astype(BF16)

    @pl.when(step == STEPS - 1)
    def _():
        rims[2] = reverse(rim_row(here[:, -SIDE:], 2)).astype(BF16)
        k = iota((2 * SIDE, 2 * SIDE), 0)
        n = iota((2 * SIDE, 2 * SIDE), 1)
        sort = hot(k, jnp.where(n < SIDE, 2 * n + 1, 2 * (n - SIDE)))
        both = jnp.concatenate([columns[0], columns[1]], axis=1).astype(BF16)
        both = dot(both, sort)
        for e in range(2):
            line = both[:, e * SIDE : (e + 1) * SIDE]
            three = jnp.concatenate([from_right(line), line, from_left(line)], axis=0).astype(BF16)
            ends[e] = three
            rim = dot(weights[2 * CH * e : 2 * CH * e + CH], three)
            if e == 0:
                rims[3] = reverse(rim).astype(BF16)
            else:
                rims[1] = rim.astype(BF16)


def first_weights(conv_first, table):
    table[...] = jnp.zeros_like(table)
    for a in range(3):
        for b in range(3):
            w = conv_first[3 * a + b].astype(F32)
            table[:, 32 * a + 8 * b : 32 * a + 8 * b + CIN] = w


def border_kernel(tile_count, direct, scal, nbr, fac, strips, comb, conv_first, *rest):
    n = tile_count - 1 if direct else 1
    arrived, rest = rest[:n], rest[n:]
    pads, rims_in, own, w_out, rest = rest[0], rest[1], rest[2], rest[3], rest[4:]
    sends, rest = rest[:n], rest[n:]
    table, w_table, lines = rest
    me = scal[0]
    first_weights(conv_first, w_table)
    w1 = w_table[...].astype(BF16)
    w_out[...] = w1
    got = take_strips(tile_count, direct, nbr, fac, me, comb, arrived, table)
    north = [reverse(got[0]), reverse(got[1]), got[2].astype(F32), got[3].astype(F32)]
    pad = [x[CH : CH + 8] for x in north]
    rims_in[0] = north[0][:CH]
    rims_in[1] = north[2][:CH]
    cols = dot(north[3][:CH].astype(BF16), ends_table(0, False))
    cols = cols + dot(north[1][:CH].astype(BF16), ends_table(0, True))
    rims_in[2] = cols[:, :SIDE]
    rims_in[3] = cols[:, SIDE:]
    pads[0] = pad[0]
    pads[1] = pad[2]
    cols = dot(pad[3].astype(BF16), ends_table(0, False)) + dot(pad[1].astype(BF16), ends_table(0, True))
    pads[2] = cols[:, :SIDE]
    pads[3] = cols[:, SIDE:]

    lane = iota((8, SIDE), 1)

    def shifted(line, first, last):
        left = jnp.where(lane == 0, first, pltpu.roll(line, 1, 1))
        right = jnp.where(lane == SIDE - 1, last, pltpu.roll(line, SIDE - 1, 1))
        return [left, line, right]

    zero = jnp.zeros((8, 1), F32)
    at = lambda x, i: x[:, i : i + 1]
    n0, e0, s0, w0 = pad
    st = [strips[i] for i in range(8)]
    across = [
        (0, [(n0, zero, zero), (st[0], at(w0, 0), at(e0, 0)), (st[1], at(w0, 1), at(e0, 1))]),
        (2, [(st[2], at(w0, 126), at(e0, 126)), (st[3], at(w0, 127), at(e0, 127)), (s0, zero, zero)]),
    ]
    along = [
        (3, [(w0, zero, zero), (st[4], at(n0, 0), at(s0, 0)), (st[5], at(n0, 1), at(s0, 1))]),
        (1, [(st[6], at(n0, 126), at(s0, 126)), (st[7], at(n0, 127), at(s0, 127)), (e0, zero, zero)]),
    ]
    lines[...] = jnp.zeros_like(lines)
    for side, three in across:
        for a, line in enumerate(three):
            for b, value in enumerate(shifted(*line)):
                lines[32 * a + 8 * b : 32 * a + 8 * b + 8, side * SIDE : (side + 1) * SIDE] = value
    for side, three in along:
        for b, line in enumerate(three):
            for a, value in enumerate(shifted(*line)):
                lines[32 * a + 8 * b : 32 * a + 8 * b + 8, side * SIDE : (side + 1) * SIDE] = value
    pre = dot(w1, lines[...].astype(BF16))
    hid = (pre * jax.nn.sigmoid(pre)).astype(BF16)
    side = lambda k: hid[:, k * SIDE : (k + 1) * SIDE]
    own[0] = side(0)
    own[1] = side(1)
    own[2] = reverse(side(2)).astype(BF16)
    own[3] = reverse(side(3)).astype(BF16)
    send_strips(tile_count, direct, nbr, me, own, sends)


def middle_kernel(tiles, pads, rims_in, w1_ref, hg, cot, prev, nxt, hidden, grad, g1, g2, planes):
    step = pl.program_id(0)

    @pl.when(step == 0)
    def _():
        g1[...] = jnp.zeros_like(g1)
        g2[...] = jnp.zeros_like(g2)
        lane = iota((8, SIDE), 1)
        rest = jnp.zeros((8, SIDE), F32)

        def put(row, line):
            planes[:, row * SIDE : (row + 1) * SIDE] = line

        def frame(line, ends):
            left = jnp.where(lane == 0, ends, pltpu.roll(line, 1, 1))
            right = jnp.where(lane == SIDE - 1, ends, pltpu.roll(line, SIDE - 1, 1))
            return jnp.concatenate([left, line, right, rest], axis=0).astype(BF16)

        put(0, frame(pads[0], rest))
        put(SIDE + 1, frame(pads[1], rest))
        for i in range(SIDE):
            back = (4 * SIDE - 2 * i - 1) % SIDE
            ends = pltpu.roll(pads[2 + i // (SIDE // 2)], back, 1)
            put(i + 1, frame(tiles[:, i * SIDE : (i + 1) * SIDE], ends))

    w1 = w1_ref[...]
    here = cot[...]
    before = jnp.where(step > 0, prev[...], jnp.zeros_like(prev))
    after = jnp.where(step < STEPS - 1, nxt[...], jnp.zeros_like(nxt))
    stacked = three_rows_down(before, here, after)
    end = is_end((CH, SIDE))
    acc1 = g1[...]
    acc2 = g2[...]
    n_rows = 4
    for p in range(ROWS // n_rows):
        base = step * ROWS + p * n_rows
        cols = []
        for a in range(3):
            lanes = pl.ds(pl.multiple_of((base + a) * SIDE, SIDE), n_rows * SIDE)
            cols.append(planes[:, lanes])
        cols = jnp.concatenate(cols, axis=0)
        pre = dot(w1, cols)
        sigma = jax.nn.sigmoid(pre)
        hid = pre * sigma
        slope = sigma * (1.0 + pre * (1.0 - sigma))
        kept, shifted, slopes = [], [], []
        for r in range(n_rows):
            row = base + r
            lanes = slice((p * n_rows + r) * SIDE, (p * n_rows + r + 1) * SIDE)
            piece = slice(r * SIDE, (r + 1) * SIDE)
            line = hg[:, lanes]
            line = line + jnp.where(end, row_ends(rims_in.at[2:4], row), 0.0)
            if p == 0 and r == 0:
                line = line + jnp.where(step == 0, rims_in[0], 0.0)
            if p == ROWS // n_rows - 1 and r == n_rows - 1:
                line = line + jnp.where(step == STEPS - 1, rims_in[1], 0.0)
            grad[:, lanes] = line.astype(BF16)
            slopes.append((line * slope[:, piece]).astype(BF16))
            h = hid[:, piece]
            hb = h.astype(BF16)
            hidden[:, lanes] = hb
            kept.append(hb)
            shifted.append((from_left(h).astype(BF16), from_right(h).astype(BF16)))
        back = jnp.concatenate(slopes, axis=1)
        acc1 = acc1 + dot_nt(back, cols)
        three = jnp.concatenate(
            [
                jnp.concatenate([x[0] for x in shifted], axis=1),
                jnp.concatenate(kept, axis=1),
                jnp.concatenate([x[1] for x in shifted], axis=1),
            ],
            axis=0,
        )
        lanes = slice(p * n_rows * SIDE, (p + 1) * n_rows * SIDE)
        acc2 = acc2 + dot_nt(stacked[:, lanes], three)
    g1[...] = acc1
    g2[...] = acc2


def close_kernel(tile_count, direct, scale, scal, nbr, fac, own, ends, top, bottom, g1, g2, fwd_w, *rest):
    n = tile_count - 1 if direct else 1
    arrived, rest = rest[:n], rest[n:]
    pads, fringe, keep, send, table, total = rest
    me = scal[0]
    got = take_strips(tile_count, direct, nbr, fac, me, own, arrived, table)
    north = reverse(got[0])
    east = reverse(got[1]).astype(BF16)
    south = got[2].astype(F32)
    west = got[3]
    pads[0] = north.astype(BF16)
    pads[1] = got[2]
    side = jnp.zeros((CH, 2 * SIDE), F32)
    for e, strip in ((0, west), (1, east)):
        three = []
        for a in range(3):
            three.append(dot(strip, ends_table(a - 1, e == 1)))
        three = jnp.concatenate(three, axis=0).astype(BF16)
        side = side + dot(fwd_w[2 * CH * e : 2 * CH * e + CH, :], three)
    fringe[0] = side[:, :SIDE]
    fringe[1] = side[:, SIDE:]
    total[:, : 3 * CH] = g2[...] * scale
    total[:, 3 * CH :] = jnp.zeros((3 * CH, CH), F32)

    def wide(line):
        return jnp.concatenate([from_left(line), line, from_right(line)], axis=0).astype(BF16)

    total[:CH, : 3 * CH] += dot_nt(top[...], wide(north)) * scale
    total[2 * CH :, : 3 * CH] += dot_nt(bottom[...], wide(south)) * scale
    total[:, :CH] += dot_nt(ends[0], west) * scale
    total[:, 2 * CH : 3 * CH] += dot_nt(ends[1], east) * scale
    first = g1[...] * scale
    for a in range(3):
        total[a * CH : (a + 1) * CH, 3 * CH : 3 * CH + 32] = first[:, 32 * a : 32 * a + 32]
    core = scal[2]
    half = keep.shape[0]
    if half == 3 * CH:
        keep[...] = total[...]
        send[...] = jnp.zeros_like(send)
    else:
        keep[...] = total[pl.ds(pl.multiple_of(core * half, 8), half), :]
        send[...] = total[pl.ds(pl.multiple_of((1 - core) * half, 8), half), :]


def pair_kernel(scal, kept, got, keep, send, total):
    total[...] = kept[...] + got[...]
    half = keep.shape[0]
    here = scal[1]
    keep[...] = total[pl.ds(pl.multiple_of(here * half, 8), half), :]
    send[...] = total[pl.ds(pl.multiple_of((1 - here) * half, 8), half), :]


def ring_kernel(tile_count, scal, mine, *rest):
    got, (out, table) = rest[:-2], rest[-2:]
    me = scal[0]
    table[me] = mine[...]
    for s in range(1, tile_count):
        table[lax.rem(me + tile_count - s, tile_count)] = got[s - 1][...]
    total = table[0]
    for t in range(1, tile_count):
        total = total + table[t]
    out[...] = total


def join_kernel(scal, mine, got, out):
    half = mine.shape[0]
    here = scal[1]
    out[pl.ds(pl.multiple_of(here * half, 8), half), :] = mine[...]
    out[pl.ds(pl.multiple_of((1 - here) * half, 8), half), :] = got[...]


def unpack(total, first, second):
    for a in range(3):
        for b in range(3):
            rows = slice(a * CH, (a + 1) * CH)
            second[3 * a + b] = total[rows, b * CH : (b + 1) * CH]
            lane = 3 * CH + 8 * b
            first[3 * a + b] = total[rows, lane : lane + CIN]


def last_kernel(scal, mine, got, first, second, total):
    half = mine.shape[0]
    here = scal[2]
    total[pl.ds(pl.multiple_of(here * half, 8), half), :] = mine[...]
    total[pl.ds(pl.multiple_of((1 - here) * half, 8), half), :] = got[...]
    unpack(total, first, second)


def output_kernel(start, hid, prev, nxt, pads, fringe, fwd_w, *rest):
    out = rest[-1]
    step = pl.program_id(0) + start
    weights = fwd_w[...]
    here = hid[...]
    before = jnp.where(step > 0, prev[...], pads[0])
    after = jnp.where(step < STEPS - 1, nxt[...], pads[1])
    up = jnp.concatenate([here[:, SIDE:], after], axis=1)
    down = jnp.concatenate([before, here[:, :-SIDE]], axis=1)
    stacked = jnp.concatenate([down, here, up], axis=0)
    end = is_end((CH, SIDE))
    for p in range(ROWS // 2):
        z = dot(weights, stacked[:, 2 * p * SIDE : (2 * p + 2) * SIDE])
        for r in range(2):
            zr = z[:, r * SIDE : (r + 1) * SIDE]
            line = zr[CH : 2 * CH] + from_left(zr[:CH]) + from_right(zr[2 * CH :])
            line = line + jnp.where(end, row_ends(fringe, step * ROWS + 2 * p + r), 0.0)
            lanes = slice((2 * p + r) * SIDE, (2 * p + r + 1) * SIDE)
            out[:, lanes] = line.astype(BF16)


def shape(dims, kind):
    return jax.ShapeDtypeStruct(dims, kind)


def row_block(offset=0):
    return pl.BlockSpec((CH, ROWS * SIDE), lambda i: (0, i + offset))


def row_before(offset=0):
    return pl.BlockSpec((CH, SIDE), lambda i: (0, jnp.maximum((i + offset) * ROWS - 1, 0)))


def row_after(offset=0):
    return pl.BlockSpec((CH, SIDE), lambda i: (0, jnp.minimum((i + offset + 1) * ROWS, SIDE - 1)))


def cost(flops, moved):
    return pl.CostEstimate(flops=int(flops), bytes_accessed=int(moved), transcendentals=0)


def whole(dims):
    return pl.BlockSpec(dims, lambda i: (0,) * len(dims))


def body(cycle_maps, send_pick, recv_pick, neighbour, facing, conv_first, conv_second, cotangent):
    map_count, _, pixel_count = cycle_maps.shape
    tile_count = lax.axis_size("tile")
    chans = lax.axis_size("chan")
    cores = lax.axis_size("sub")
    direct = tile_count == 4
    assert map_count == 1 and pixel_count == PIX and tile_count != 8
    slots = send_pick.shape[0]
    per_pair = slots // tile_count // LOW
    groups = slots // LOW
    scal = jnp.stack([lax.axis_index(n).astype(jnp.int32) for n in ("tile", "chan", "sub")])
    cyc = cycle_maps.reshape(CIN, PIX)
    cot = cotangent.reshape(CH, PIX)
    n_send = tile_count - 1 if direct else 1

    def exchange(sends):
        if direct:
            return [
                lax.ppermute(x, "tile", [(i, (i + s) % tile_count) for i in range(tile_count)])
                for s, x in zip(range(1, tile_count), sends)
            ]
        return [lax.all_to_all(sends[0], "tile", 0, 0, tiled=True)]

    def sent(dims, kind):
        if direct:
            return [shape(dims, kind)] * n_send
        return [shape((tile_count,) + dims, kind)]

    if direct:
        block_shapes = [shape((CIN, per_pair, LOW), BF16)] * tile_count
    else:
        block_shapes = [shape((tile_count, CIN, per_pair, LOW), BF16)]
    blocks = pl.pallas_call(
        functools.partial(send_kernel, tile_count, direct),
        in_specs=[SMEM, VMEM, VMEM],
        out_specs=[VMEM] * len(block_shapes),
        out_shape=block_shapes,
        scratch_shapes=[
            pltpu.VMEM((CIN * PIX // LOW, LOW), F32),
            pltpu.VMEM((CIN * PIX // LOW, LOW), BF16),
            pltpu.VMEM((CIN, groups, LOW), F32),
        ],
        compiler_params=tile_params(16),
        name="send_pick",
    )(scal, cyc, send_pick.reshape(slots // SIDE, SIDE))
    if direct:
        blocks = [blocks[0]] + exchange(blocks[1:])
    else:
        blocks = exchange(blocks)

    hg, rims, ends, fwd_w = pl.pallas_call(
        frame_kernel,
        grid=(STEPS,),
        in_specs=[row_block(), row_before(), row_after(), whole((9, CH, CH))],
        out_specs=[row_block(), whole((4, CH, SIDE)), whole((2, 3 * CH, SIDE)), whole((3 * CH, 3 * CH))],
        out_shape=[
            shape((CH, PIX), F32),
            shape((4, CH, SIDE), BF16),
            shape((2, 3 * CH, SIDE), BF16),
            shape((3 * CH, 3 * CH), BF16),
        ],
        scratch_shapes=[pltpu.VMEM((3 * CH, 3 * CH), BF16), pltpu.VMEM((2, CH, SIDE), F32)],
        compiler_params=tile_params(32),
        cost_estimate=cost(2 * 9 * CH * CH * PIX, 6 * CH * PIX),
        name="frame",
    )(cot, cot, cot, conv_second)

    index = recv_pick.reshape(SIDE, SIDE)
    *sends, source, strips, comb = pl.pallas_call(
        functools.partial(strip_kernel, tile_count, direct),
        in_specs=[SMEM, SMEM] + [VMEM] * (2 + len(blocks)),
        out_specs=[VMEM] * (n_send + 3),
        out_shape=sent((COMB, SIDE), BF16)
        + [shape((CIN * groups, LOW), BF16), shape((8, 8, SIDE), F32), shape((4, COMB, SIDE), BF16)],
        scratch_shapes=[pltpu.VMEM((CIN * groups, LOW), F32)],
        compiler_params=tile_params(16),
        name="strips",
    )(scal, neighbour, index, rims, *blocks)
    arrived = exchange(sends)

    tiles = pl.pallas_call(
        functools.partial(main_pick_kernel, groups),
        in_specs=[VMEM] * 2,
        out_specs=VMEM,
        out_shape=shape((8, PIX), F32),
        compiler_params=tile_params(16),
        cost_estimate=cost(2 * CIN * groups * LOW * PIX, 2 * 8 * PIX),
        name="recv_pick",
    )(index, source)

    pads, rims_in, own, w1, *sends = pl.pallas_call(
        functools.partial(border_kernel, tile_count, direct),
        in_specs=[SMEM] * 3 + [VMEM] * (3 + n_send),
        out_specs=[VMEM] * (4 + n_send),
        out_shape=[
            shape((4, 8, SIDE), F32),
            shape((4, CH, SIDE), F32),
            shape((4, CH, SIDE), BF16),
            shape((CH, 96), BF16),
        ]
        + sent((CH, SIDE), BF16),
        scratch_shapes=[
            pltpu.VMEM((5 + tile_count, COMB, SIDE), BF16),
            pltpu.VMEM((CH, 96), F32),
            pltpu.VMEM((96, 4 * SIDE), F32),
        ],
        compiler_params=tile_params(16),
        name="border",
    )(scal, neighbour, facing, strips, comb, conv_first, *arrived)
    arrived = exchange(sends)

    hidden, grad, g1, g2 = pl.pallas_call(
        middle_kernel,
        grid=(STEPS,),
        in_specs=[
            whole((8, PIX)),
            whole((4, 8, SIDE)),
            whole((4, CH, SIDE)),
            whole((CH, 96)),
            row_block(),
            row_block(),
            row_before(),
            row_after(),
        ],
        out_specs=[row_block(), row_block(), whole((CH, 96)), whole((3 * CH, 3 * CH))],
        out_shape=[
            shape((CH, PIX), BF16),
            shape((CH, PIX), BF16),
            shape((CH, 96), F32),
            shape((3 * CH, 3 * CH), F32),
        ],
        scratch_shapes=[pltpu.VMEM((32, (SIDE + 2) * SIDE), BF16)],
        compiler_params=tile_params(40),
        cost_estimate=cost(2 * 9 * CH * CH * PIX, 12 * CH * PIX),
        name="middle",
    )(tiles, pads, rims_in, w1, hg, cot, cot, cot)

    scale = 1.0 / math.sqrt(map_count * chans * cores * tile_count * PIX)
    fast_sum = direct and chans == 2 and cores == 2
    half = 3 * CH // 2 if fast_sum else 3 * CH
    top = pl.BlockSpec((CH, SIDE), lambda i: (0, 0))
    bottom = pl.BlockSpec((CH, SIDE), lambda i: (0, SIDE - 1))
    smem = pl.BlockSpec(memory_space=pltpu.SMEM)
    pads2, fringe, keep, send = pl.pallas_call(
        functools.partial(close_kernel, tile_count, direct, scale),
        grid=(1,),
        in_specs=[smem, smem, smem, whole((4, CH, SIDE)), whole((2, 3 * CH, SIDE)), top, bottom]
        + [whole((CH, 96)), whole((3 * CH, 3 * CH)), whole((3 * CH, 3 * CH))]
        + [whole(x.shape) for x in arrived],
        out_specs=[whole((2, CH, SIDE)), whole((2, CH, SIDE)), whole((half, LOW)), whole((half, LOW))],
        out_shape=[
            shape((2, CH, SIDE), BF16),
            shape((2, CH, SIDE), F32),
            shape((half, LOW), F32),
            shape((half, LOW), F32),
        ],
        scratch_shapes=[pltpu.VMEM((5 + tile_count, CH, SIDE), BF16), pltpu.VMEM((3 * CH, LOW), F32)],
        compiler_params=tile_params(16),
        name="close",
    )(scal, neighbour, facing, own, ends, cot, cot, g1, g2, fwd_w, *arrived)

    def convolve(start, count, out):
        steps = [] if out is None else [out]
        return pl.pallas_call(
            functools.partial(output_kernel, start),
            grid=(count,),
            in_specs=[
                row_block(start),
                row_before(start),
                row_after(start),
                whole((2, CH, SIDE)),
                whole((2, CH, SIDE)),
                whole((3 * CH, 3 * CH)),
            ]
            + [pl.BlockSpec(memory_space=pl.ANY)] * len(steps),
            out_specs=row_block(start),
            out_shape=shape((CH, PIX), BF16),
            input_output_aliases={6: 0} if steps else {},
            compiler_params=tile_params(32),
            cost_estimate=cost(2 * 9 * CH * CH * PIX * count // STEPS, 4 * CH * PIX * count // STEPS),
            name="output",
        )(hidden, hidden, hidden, pads2, fringe, fwd_w, *steps)

    finals = [shape((9, CH, CIN), F32), shape((9, CH, CH), F32)]
    if fast_sum:
        swap = lambda x, name: lax.ppermute(x, name, [(0, 1), (1, 0)])
        quarter = half // 2
        got = swap(send, "sub")
        out = convolve(0, 2, None)
        keep2, send2 = pl.pallas_call(
            pair_kernel,
            in_specs=[SMEM, VMEM, VMEM],
            out_specs=[VMEM, VMEM],
            out_shape=[shape((quarter, LOW), F32)] * 2,
            scratch_shapes=[pltpu.VMEM((half, LOW), F32)],
            name="pair",
        )(scal, keep, got)
        got = swap(send2, "chan")
        out = convolve(2, 2, out)
        mine = keep2 + got
        got = exchange([mine] * n_send)
        out = convolve(4, 4, out)
        mine = pl.pallas_call(
            functools.partial(ring_kernel, tile_count),
            in_specs=[SMEM] + [VMEM] * tile_count,
            out_specs=VMEM,
            out_shape=shape((quarter, LOW), F32),
            scratch_shapes=[pltpu.VMEM((tile_count, quarter, LOW), F32)],
            name="ring",
        )(scal, mine, *got)
        got = swap(mine, "chan")
        mine = pl.pallas_call(
            join_kernel,
            in_specs=[SMEM, VMEM, VMEM],
            out_specs=VMEM,
            out_shape=shape((half, LOW), F32),
            name="join",
        )(scal, mine, got)
        got = swap(mine, "sub")
        first, second = pl.pallas_call(
            last_kernel,
            in_specs=[SMEM, VMEM, VMEM],
            out_specs=[VMEM, VMEM],
            out_shape=finals,
            scratch_shapes=[pltpu.VMEM((3 * CH, LOW), F32)],
            name="last",
        )(scal, mine, got)
    else:
        out = convolve(0, STEPS, None)
        total = lax.psum(keep, ("tile", "chan", "sub"))
        first, second = pl.pallas_call(
            unpack, in_specs=[VMEM], out_specs=[VMEM, VMEM], out_shape=finals, name="unpack"
        )(total)
    return (out.reshape(1, CH, PIX), grad.reshape(1, CH, PIX), first, second)


def solution(mesh):
    in_specs = (
        P(("groups", "chan", "sub"), None, "tile"),
        P("tile"),
        P("tile"),
        P(),
        P(),
        P(),
        P(),
        P(("groups", "chan", "sub"), None, "tile"),
    )
    out_specs = (
        P(("groups", "chan", "sub"), None, "tile"),
        P(("groups", "chan", "sub"), None, "tile"),
        P("groups", None, None),
        P("groups", None, None),
    )
    return jax.shard_map(body, mesh=mesh, in_specs=in_specs, out_specs=out_specs, check_vma=False)
```

```python
import functools
import math

import jax
import jax.numpy as jnp
from jax import lax
from jax.experimental import pallas as pl
from jax.experimental.pallas import tpu as pltpu
from jax.sharding import PartitionSpec as P

SIDE = 128
PIX = SIDE * SIDE
CH = 64
CIN = 3
LOW = 256
COMB = 96
ROWS = 16
STEPS = SIDE // ROWS
F32 = jnp.float32
BF16 = jnp.bfloat16
SMEM = pl.BlockSpec(memory_space=pltpu.SMEM)
VMEM = pl.BlockSpec(memory_space=pltpu.VMEM)


def iota(shape, dim):
    return lax.broadcasted_iota(jnp.int32, shape, dim)


def hot(a, b):
    return jnp.where(a == b, 1.0, 0.0).astype(BF16)


def dot(a, b):
    return jnp.dot(a, b, preferred_element_type=F32)


def dot_nt(a, b):
    return lax.dot_general(a, b, (((1,), (1,)), ((), ())), preferred_element_type=F32)


def reverse(strip):
    swap = hot(iota((SIDE, SIDE), 0) + iota((SIDE, SIDE), 1), SIDE - 1)
    return dot(strip.astype(BF16), swap)


def from_left(x):
    return jnp.where(iota(x.shape, 1) == 0, 0.0, pltpu.roll(x, 1, 1))


def from_right(x):
    return jnp.where(iota(x.shape, 1) == SIDE - 1, 0.0, pltpu.roll(x, SIDE - 1, 1))


def ends_table(shift, east):
    src = iota((SIDE, 2 * SIDE), 0)
    lane = iota((SIDE, 2 * SIDE), 1)
    return hot(lane, 2 * (src - shift) + (0 if east else 1))


def row_ends(pairs, row):
    half = row // (SIDE // 2)
    back = lax.rem(4 * SIDE - 2 * row - 1, SIDE)
    return pltpu.roll(pairs[half], back, 1)


def is_end(shape):
    lane = iota(shape, 1)
    return (lane == 0) | (lane == SIDE - 1)


def pick_rows(low_rows, high_rows, groups, source):
    found = dot(source, hot(iota((LOW, LOW), 0), low_rows))
    lines = iota((8, LOW), 0)
    accs = [jnp.zeros((8, LOW), F32)] * CIN
    for g in range(groups // 8):
        here = lines == high_rows - 8 * g
        for c in range(CIN):
            at = c * groups + 8 * g
            accs[c] = jnp.where(here, found[at : at + 8], accs[c])
    return [jnp.sum(x, axis=0, keepdims=True) for x in accs]


def split_index(index):
    return index & (LOW - 1), index >> 8


def tile_params(limit_mib):
    return pltpu.CompilerParams(vmem_limit_bytes=limit_mib << 20)


def send_kernel(tile_count, direct, scal, cyc, index, *rest):
    outs, (stage, source, found) = rest[:-3], rest[-3:]
    groups = PIX // LOW
    per_dest = index.shape[0] // 2 // tile_count
    whole = cyc[...].astype(F32)
    for h in range(groups):
        piece = whole[:, h * LOW : (h + 1) * LOW]
        for c in range(CIN):
            stage[pl.ds(c * groups + h, 1), :] = piece[c : c + 1]
    source[...] = stage[...].astype(BF16)
    data = source[...]
    me = scal[0]

    def chunk(m, carry):
        if direct:
            dest = me ^ (m // per_dest)
            at = dest * per_dest + lax.rem(m, per_dest)
        else:
            at = m
        row = jnp.concatenate([index[pl.ds(2 * at, 1), :], index[pl.ds(2 * at + 1, 1), :]], axis=1)
        low, high = split_index(row)
        picked = pick_rows(low, high, groups, data)
        for c in range(CIN):
            found[c, pl.ds(m, 1), :] = picked[c]
        return carry

    lax.fori_loop(0, tile_count * per_dest, chunk, 0, unroll=4)
    for d in range(tile_count):
        for c in range(CIN):
            block = found[c, d * per_dest : (d + 1) * per_dest, :].astype(BF16)
            if direct:
                outs[d][c] = block
            else:
                outs[0][d, c] = block


def side_towards(nbr, me, dest):
    side = jnp.int32(0)
    for k in range(4):
        side = jnp.where(nbr[me, k] == dest, k, side)
    return side


def send_strips(tile_count, direct, nbr, me, strips, outs):
    if direct:
        for s in range(1, tile_count):
            dest = me ^ s
            outs[s - 1][...] = strips[side_towards(nbr, me, dest)]
    else:
        for dest in range(tile_count):
            outs[0][dest] = strips[side_towards(nbr, me, dest)]


def take_strips(tile_count, direct, nbr, fac, me, own, arrived, table):
    for k in range(4):
        table[k] = own[k]
    if direct:
        for s in range(1, tile_count):
            table[4 + (me ^ s)] = arrived[s - 1][...]
    else:
        for d in range(tile_count):
            table[4 + d] = arrived[0][d]
    table[4 + tile_count] = jnp.zeros(table.shape[1:], table.dtype)
    got = []
    for k in range(4):
        other = nbr[me, k]
        at = jnp.where(other == me, fac[me, k], 4 + other)
        at = jnp.where(other < 0, 4 + tile_count, at)
        got.append(table[at])
    return got


def side_ends(north, east, south, west):
    at = lambda x, i: x[:, i : i + 1]
    last = SIDE - 1
    fours = [
        (at(west, 0), at(east, 0), at(west, 1), at(east, 1)),
        (at(north, last), at(south, last), at(north, last - 1), at(south, last - 1)),
        (at(east, last), at(west, last), at(east, last - 1), at(west, last - 1)),
        (at(south, 0), at(north, 0), at(south, 1), at(north, 1)),
    ]
    lane = iota((8, SIDE), 1)
    lines = []
    for four in fours:
        line = jnp.zeros((8, SIDE), F32)
        for n, value in enumerate(four):
            line = jnp.where(lane == n, value, line)
        lines.append(line)
    return lines


def strip_kernel(tile_count, direct, scal, nbr, fac, index, rims, *rest):
    n_in = tile_count if direct else 1
    n_out = tile_count - 1 if direct else 1
    blocks, rest = rest[:n_in], rest[n_in:]
    sends, rest = rest[:n_out], rest[n_out:]
    source, strips, comb, stage = rest
    me = scal[0]
    per_src = blocks[0].shape[-2]
    groups = tile_count * per_src
    for s in range(tile_count):
        for c in range(CIN):
            if direct:
                src = me ^ s
                at = c * groups + src * per_src
                if per_src % 8 == 0:
                    at = pl.multiple_of(at, 8)
                stage[pl.ds(at, per_src), :] = blocks[s][c].astype(F32)
            else:
                at = c * groups + s * per_src
                stage[at : at + per_src, :] = blocks[0][s, c].astype(F32)
    source[...] = stage[...].astype(BF16)
    data = source[...]
    flipped = index[...].astype(F32).T
    col = lambda j: flipped[j : j + 1, :].astype(jnp.int32)
    row = lambda i: index[i : i + 1, :]
    pairs = [(row(0), row(1)), (row(126), row(127)), (col(0), col(1)), (col(126), col(127))]
    for n, pair in enumerate(pairs):
        low, high = split_index(jnp.concatenate(pair, axis=1))
        picked = pick_rows(low, high, groups, data)
        for c in range(CIN):
            strips[2 * n, c : c + 1, :] = picked[c][:, :SIDE]
            strips[2 * n + 1, c : c + 1, :] = picked[c][:, SIDE:]
    for n in range(8):
        strips[n, CIN:, :] = jnp.zeros((8 - CIN, SIDE), F32)
    edge = [strips[0], strips[7], reverse(strips[3]), reverse(strips[4])]
    inner = [strips[1], strips[6], reverse(strips[2]), reverse(strips[5])]
    blank = jnp.zeros((COMB - CH - 16, SIDE), F32)
    for k in range(4):
        comb[k, :CH, :] = rims[k]
        comb[k, CH:, :] = jnp.concatenate([edge[k], inner[k], blank], axis=0).astype(BF16)
    if direct:
        pads = []
        for k in range(4):
            mine = comb[jnp.where(nbr[me, k] == me, fac[me, k], 0), CH : CH + 16, :].astype(F32)[:8]
            mine = jnp.where(nbr[me, k] == me, mine, 0.0)
            pads.append(reverse(mine) if k < 2 else mine)
        blank = jnp.zeros((8, SIDE), F32)
        for k, line in enumerate(side_ends(*pads)):
            comb[k, CH + 16 :, :] = jnp.concatenate([line, blank], axis=0).astype(BF16)
    send_strips(tile_count, direct, nbr, me, comb, sends)


def main_pick_kernel(groups, index, source, out):
    data = source[...]

    def chunk(m, carry):
        row = jnp.concatenate([index[pl.ds(2 * m, 1), :], index[pl.ds(2 * m + 1, 1), :]], axis=1)
        low, high = split_index(row)
        picked = pick_rows(low, high, groups, data)
        lanes = pl.ds(pl.multiple_of(m * LOW, LOW), LOW)
        for c in range(CIN):
            out[c : c + 1, lanes] = picked[c]
        return carry

    lax.fori_loop(0, PIX // LOW, chunk, 0, unroll=4)
    out[CIN:, :] = jnp.zeros((8 - CIN, PIX), F32)


def edge_kernel(cot, conv_second, conv_first, rims, columns, fwd_w, back_w, w1, side_w, acc, table):
    step = pl.program_id(0)

    @pl.when(step == 0)
    def _():
        for a in range(3):
            for b in range(3):
                w = conv_second[3 * a + b]
                fwd_w[b * CH : (b + 1) * CH, a * CH : (a + 1) * CH] = w
                back_w[a * CH : (a + 1) * CH, b * CH : (b + 1) * CH] = w.astype(F32).T.astype(BF16)
        table[...] = jnp.zeros_like(table)
        for side in range(4):
            for t in range(3):
                for u in range(3):
                    p = [3 * t + u, 3 * u + 2 - t, 3 * (2 - t) + 2 - u, 3 * (2 - u) + t][side]
                    table[32 * t + 8 * u : 32 * t + 8 * u + CIN, :CH] = conv_first[p].astype(F32)
            side_w[side] = table[...].T[:CH, : 3 * 32].astype(BF16)
        w1[...] = side_w[0]
        acc[...] = jnp.zeros_like(acc)

    half = step // (STEPS // 2)
    got = acc[half]
    pair = iota((CH, SIDE), 1) // 2
    for t in range(ROWS):
        r = step * ROWS + t
        line = cot[:, t * SIDE : (t + 1) * SIDE].astype(F32)
        turned = pltpu.roll(line, lax.rem(2 * r + 1, SIDE), 1)
        got = jnp.where(pair == lax.rem(r, SIDE // 2), turned, got)
    acc[half] = got

    def rim_row(line, a):
        line = line.astype(F32)
        three = jnp.concatenate([from_right(line), line, from_left(line)], axis=0).astype(BF16)
        return dot(back_w[a * CH : (a + 1) * CH, :], three)

    @pl.when(step == 0)
    def _():
        rims[0] = rim_row(cot[:, :SIDE], 0).astype(BF16)

    @pl.when(step == STEPS - 1)
    def _():
        rims[2] = reverse(rim_row(cot[:, (ROWS - 1) * SIDE :], 2)).astype(BF16)
        k = iota((2 * SIDE, 2 * SIDE), 0)
        n = iota((2 * SIDE, 2 * SIDE), 1)
        sort = hot(k, jnp.where(n < SIDE, 2 * n + 1, 2 * (n - SIDE)))
        both = jnp.concatenate([acc[0], acc[1]], axis=1).astype(BF16)
        both = dot(both, sort)
        for e in range(2):
            line = both[:, e * SIDE : (e + 1) * SIDE]
            columns[e] = line.astype(BF16)
            rim = jnp.zeros((CH, SIDE), F32)
            for a, near in enumerate((from_right(line), line, from_left(line))):
                w = back_w[a * CH : (a + 1) * CH, 2 * e * CH : (2 * e + 1) * CH]
                rim = rim + dot(w, near.astype(BF16))
            if e == 0:
                rims[3] = reverse(rim).astype(BF16)
            else:
                rims[1] = rim.astype(BF16)


def shifted(line, first, last):
    lane = iota(line.shape, 1)
    left = jnp.where(lane == 0, first, pltpu.roll(line, 1, 1))
    right = jnp.where(lane == SIDE - 1, last, pltpu.roll(line, SIDE - 1, 1))
    return [left, line, right]


def deliver(got, pads, rims_in):
    north = [reverse(got[0]), reverse(got[1]), got[2].astype(F32), got[3].astype(F32)]
    pad = [x[CH : CH + 8] for x in north]
    rims_in[0] = north[0][:CH]
    rims_in[1] = north[2][:CH]
    cols = dot(north[3][:CH].astype(BF16), ends_table(0, False))
    cols = cols + dot(north[1][:CH].astype(BF16), ends_table(0, True))
    rims_in[2] = cols[:, :SIDE]
    rims_in[3] = cols[:, SIDE:]
    pads[0] = pad[0]
    pads[1] = pad[2]
    cols = dot(pad[3].astype(BF16), ends_table(0, False)) + dot(pad[1].astype(BF16), ends_table(0, True))
    pads[2] = cols[:, :SIDE]
    pads[3] = cols[:, SIDE:]
    return pad


def near_kernel(tile_count, scal, nbr, fac, strips, comb, side_w, *rest):
    n = tile_count - 1
    arrived, (pads, rims_in, incoming, table, ends, lines) = rest[:n], rest[n:]
    me = scal[0]
    got = take_strips(tile_count, True, nbr, fac, me, comb, arrived, table)
    pad = deliver(got, pads, rims_in)
    for k, line in enumerate(side_ends(*pad)):
        ends[k] = line
    lines[...] = jnp.zeros_like(lines)
    zero = jnp.zeros((8, 1), F32)
    for k in range(4):
        other, face = nbr[me, k], fac[me, k]
        there = got[k][CH:].astype(F32)
        end = jnp.where(other == me, ends[face], there[16:24])
        at = lambda i: end[:, i : i + 1]
        outer = reverse(comb[k, CH : CH + 16, :])[:8]
        three = [(outer, zero, zero), (there[:8], at(0), at(1)), (there[8:16], at(2), at(3))]
        for t, line in enumerate(three):
            for u, value in enumerate(shifted(*line)):
                lines[32 * t + 8 * u : 32 * t + 8 * u + 8, :] = value
        pre = dot(side_w[face], lines[...].astype(BF16))
        hid = jnp.where(other < 0, 0.0, pre * jax.nn.sigmoid(pre))
        incoming[k] = (reverse(hid) if k < 2 else hid).astype(BF16)


def border_kernel(tile_count, scal, nbr, fac, strips, comb, w1_ref, arrived, *rest):
    pads, rims_in, own, sends, table, lines = rest
    me = scal[0]
    w1 = w1_ref[...]
    got = take_strips(tile_count, False, nbr, fac, me, comb, [arrived], table)
    pad = deliver(got, pads, rims_in)
    zero = jnp.zeros((8, 1), F32)
    at = lambda x, i: x[:, i : i + 1]
    n0, e0, s0, w0 = pad
    st = [strips[i] for i in range(8)]
    across = [
        (0, [(n0, zero, zero), (st[0], at(w0, 0), at(e0, 0)), (st[1], at(w0, 1), at(e0, 1))]),
        (2, [(st[2], at(w0, 126), at(e0, 126)), (st[3], at(w0, 127), at(e0, 127)), (s0, zero, zero)]),
    ]
    along = [
        (3, [(w0, zero, zero), (st[4], at(n0, 0), at(s0, 0)), (st[5], at(n0, 1), at(s0, 1))]),
        (1, [(st[6], at(n0, 126), at(s0, 126)), (st[7], at(n0, 127), at(s0, 127)), (e0, zero, zero)]),
    ]
    lines[...] = jnp.zeros_like(lines)
    for side, three in across:
        for a, line in enumerate(three):
            for b, value in enumerate(shifted(*line)):
                lines[32 * a + 8 * b : 32 * a + 8 * b + 8, side * SIDE : (side + 1) * SIDE] = value
    for side, three in along:
        for b, line in enumerate(three):
            for a, value in enumerate(shifted(*line)):
                lines[32 * a + 8 * b : 32 * a + 8 * b + 8, side * SIDE : (side + 1) * SIDE] = value
    pre = dot(w1, lines[...].astype(BF16))
    hid = (pre * jax.nn.sigmoid(pre)).astype(BF16)
    side = lambda k: hid[:, k * SIDE : (k + 1) * SIDE]
    own[0] = side(0)
    own[1] = side(1)
    own[2] = reverse(side(2)).astype(BF16)
    own[3] = reverse(side(3)).astype(BF16)
    send_strips(tile_count, False, nbr, me, own, [sends])


def middle_kernel(tiles, pads, rims_in, w1_ref, back_w, cot, prev, nxt, hidden, grad, g1, g2, planes, near, spread, kept):
    step = pl.program_id(0)

    @pl.when(step == 0)
    def _():
        g1[...] = jnp.zeros_like(g1)
        g2[...] = jnp.zeros_like(g2)
        kept[:, : 2 * SIDE] = jnp.zeros((CH, 2 * SIDE), BF16)
        rest = jnp.zeros((8, SIDE), F32)

        def put(row, line, ends):
            three = shifted(line, ends, ends)
            planes[:, row * SIDE : (row + 1) * SIDE] = jnp.concatenate(three + [rest], axis=0).astype(BF16)

        put(0, pads[0], rest)
        put(SIDE + 1, pads[1], rest)
        for i in range(SIDE):
            back = (4 * SIDE - 2 * i - 1) % SIDE
            ends = pltpu.roll(pads[2 + i // (SIDE // 2)], back, 1)
            put(i + 1, tiles[:, i * SIDE : (i + 1) * SIDE], ends)

    w1 = w1_ref[...]
    weights = back_w[...]
    for t in range(ROWS + 2):
        if t == 0:
            line = jnp.where(step > 0, prev[...], jnp.zeros_like(prev))
        elif t == ROWS + 1:
            line = jnp.where(step < STEPS - 1, nxt[...], jnp.zeros_like(nxt))
        else:
            line = cot[:, (t - 1) * SIDE : t * SIDE]
        lanes = slice(t * SIDE, (t + 1) * SIDE)
        wide = line.astype(F32)
        near[:CH, lanes] = from_right(wide).astype(BF16)
        near[CH : 2 * CH, lanes] = line
        near[2 * CH :, lanes] = from_left(wide).astype(BF16)
    for p in range((ROWS + 2) // 2):
        lanes = slice(2 * p * SIDE, (2 * p + 2) * SIDE)
        spread[:, lanes] = dot(weights, near[:, lanes])
    end = is_end((CH, SIDE))
    n_rows = 4
    acc1 = g1[...]
    for p in range(ROWS // n_rows):
        base = step * ROWS + p * n_rows
        cols = []
        for a in range(3):
            lanes = pl.ds(pl.multiple_of((base + a) * SIDE, SIDE), n_rows * SIDE)
            cols.append(planes[:, lanes])
        cols = jnp.concatenate(cols, axis=0)
        pre = dot(w1, cols)
        sigma = jax.nn.sigmoid(pre)
        hid = pre * sigma
        slope = sigma * (1.0 + pre * (1.0 - sigma))
        slopes = []
        for r in range(n_rows):
            t = p * n_rows + r
            here = lambda a: slice((t + 2 - a) * SIDE, (t + 3 - a) * SIDE)
            line = spread[:CH, here(0)] + spread[CH : 2 * CH, here(1)] + spread[2 * CH :, here(2)]
            line = line + jnp.where(end, row_ends(rims_in.at[2:4], base + r), 0.0)
            if t == 0:
                line = line + jnp.where(step == 0, rims_in[0], 0.0)
            if t == ROWS - 1:
                line = line + jnp.where(step == STEPS - 1, rims_in[1], 0.0)
            grad[:, t * SIDE : (t + 1) * SIDE] = line.astype(BF16)
            slopes.append((line * slope[:, r * SIDE : (r + 1) * SIDE]).astype(BF16))
        lanes = slice(p * n_rows * SIDE, (p + 1) * n_rows * SIDE)
        hid = hid.astype(BF16)
        hidden[:, lanes] = hid
        kept[:, (p * n_rows + 2) * SIDE : ((p + 1) * n_rows + 2) * SIDE] = hid
        acc1 = acc1 + dot_nt(cols, jnp.concatenate(slopes, axis=1))
    g1[...] = acc1

    def weigh(first, count):
        three = [kept[:, (first + a) * SIDE : (first + a + count) * SIDE] for a in range(3)]
        return dot_nt(near[:, first * SIDE : (first + count) * SIDE], jnp.concatenate(three, axis=0))

    g2[...] += weigh(0, ROWS)

    @pl.when(step == STEPS - 1)
    def _():
        kept[:, (ROWS + 2) * SIDE :] = jnp.zeros((CH, SIDE), BF16)
        g2[...] += weigh(ROWS, 1)

    kept[:, : 2 * SIDE] = kept[:, ROWS * SIDE : (ROWS + 2) * SIDE]


def close_kernel(tile_count, direct, scale, scal, nbr, fac, columns, top, bottom, g1, g2, fwd_w, *rest):
    if direct:
        incoming, pads, fringe, keep, send, total = rest
        north, east, south, west = [incoming[k] for k in range(4)]
    else:
        own, arrived, pads, fringe, keep, send, total, table = rest
        got = take_strips(tile_count, direct, nbr, fac, scal[0], own, [arrived], table)
        north, east = reverse(got[0]).astype(BF16), reverse(got[1]).astype(BF16)
        south, west = got[2], got[3]
    pads[0] = north
    pads[1] = south
    side = jnp.zeros((CH, 2 * SIDE), F32)
    for e, strip in ((0, west), (1, east)):
        three = [dot(strip, ends_table(a - 1, e == 1)) for a in range(3)]
        three = jnp.concatenate(three, axis=0).astype(BF16)
        side = side + dot(fwd_w[2 * CH * e : 2 * CH * e + CH, :], three)
    fringe[0] = side[:, :SIDE]
    fringe[1] = side[:, SIDE:]
    total[:, : 3 * CH] = g2[...] * scale
    total[:, 3 * CH :] = jnp.zeros((3 * CH, CH), F32)
    total[: 3 * 32, 3 * CH :] = g1[...] * scale

    def three_ways(line, turned):
        line = line.astype(F32)
        ways = [from_right(line), line, from_left(line)]
        return jnp.concatenate(ways[::-1] if turned else ways, axis=0).astype(BF16)

    total[:, :CH] += dot_nt(three_ways(top[...], False), north) * scale
    total[:, 2 * CH : 3 * CH] += dot_nt(three_ways(bottom[...], False), south) * scale
    total[:CH, : 3 * CH] += dot_nt(columns[0], three_ways(west, True)) * scale
    total[2 * CH :, : 3 * CH] += dot_nt(columns[1], three_ways(east, True)) * scale
    core = scal[2]
    half = keep.shape[0]
    if half == 3 * CH:
        keep[...] = total[...]
        send[...] = jnp.zeros_like(send)
    else:
        keep[...] = total[pl.ds(pl.multiple_of(core * half, 8), half), :]
        send[...] = total[pl.ds(pl.multiple_of((1 - core) * half, 8), half), :]


def pair_kernel(scal, kept, got, after, keep, send, total):
    total[...] = kept[...] + got[...]
    half = keep.shape[0]
    here = scal[1]
    keep[...] = total[pl.ds(pl.multiple_of(here * half, 8), half), :]
    send[...] = total[pl.ds(pl.multiple_of((1 - here) * half, 8), half), :]


def ring_kernel(tile_count, scal, mine, *rest):
    got, (after, out, table) = rest[:-3], rest[-3:]
    me = scal[0]
    table[me] = mine[...]
    for s in range(1, tile_count):
        table[me ^ s] = got[s - 1][...]
    total = table[0]
    for t in range(1, tile_count):
        total = total + table[t]
    out[...] = total


def join_kernel(scal, mine, got, after, out):
    half = mine.shape[0]
    here = scal[1]
    out[pl.ds(pl.multiple_of(here * half, 8), half), :] = mine[...]
    out[pl.ds(pl.multiple_of((1 - here) * half, 8), half), :] = got[...]


def unpack(total, first, second):
    for a in range(3):
        for b in range(3):
            second[3 * a + b] = total[b * CH : (b + 1) * CH, a * CH : (a + 1) * CH]
            row = 32 * a + 8 * b
            first[3 * a + b] = total[row : row + CIN, 3 * CH :]


def last_kernel(scal, mine, got, first, second, total):
    half = mine.shape[0]
    here = scal[2]
    total[pl.ds(pl.multiple_of(here * half, 8), half), :] = mine[...]
    total[pl.ds(pl.multiple_of((1 - here) * half, 8), half), :] = got[...]
    unpack(total, first, second)


def output_kernel(start, hid, prev, nxt, pads, fringe, fwd_w, *rest):
    out, token = rest[-2:]
    token[...] = jnp.zeros_like(token)
    step = pl.program_id(0) + start
    weights = fwd_w[...]
    here = hid[...]
    before = jnp.where(step > 0, prev[...], pads[0])
    after = jnp.where(step < STEPS - 1, nxt[...], pads[1])
    up = jnp.concatenate([here[:, SIDE:], after], axis=1)
    down = jnp.concatenate([before, here[:, :-SIDE]], axis=1)
    stacked = jnp.concatenate([down, here, up], axis=0)
    end = is_end((CH, SIDE))
    for p in range(ROWS // 2):
        z = dot(weights, stacked[:, 2 * p * SIDE : (2 * p + 2) * SIDE])
        for r in range(2):
            zr = z[:, r * SIDE : (r + 1) * SIDE]
            line = zr[CH : 2 * CH] + from_left(zr[:CH]) + from_right(zr[2 * CH :])
            line = line + jnp.where(end, row_ends(fringe, step * ROWS + 2 * p + r), 0.0)
            lanes = slice((2 * p + r) * SIDE, (2 * p + r + 1) * SIDE)
            out[:, lanes] = line.astype(BF16)


def shape(dims, kind):
    return jax.ShapeDtypeStruct(dims, kind)


def row_block(offset=0):
    return pl.BlockSpec((CH, ROWS * SIDE), lambda i: (0, i + offset))


def row_before(offset=0):
    return pl.BlockSpec((CH, SIDE), lambda i: (0, jnp.maximum((i + offset) * ROWS - 1, 0)))


def row_after(offset=0):
    return pl.BlockSpec((CH, SIDE), lambda i: (0, jnp.minimum((i + offset + 1) * ROWS, SIDE - 1)))


def cost(flops, moved):
    return pl.CostEstimate(flops=int(flops), bytes_accessed=int(moved), transcendentals=0)


def whole(dims):
    return pl.BlockSpec(dims, lambda i: (0,) * len(dims))


def body(cycle_maps, send_pick, recv_pick, neighbour, facing, conv_first, conv_second, cotangent):
    map_count, _, pixel_count = cycle_maps.shape
    tile_count = lax.axis_size("tile")
    chans = lax.axis_size("chan")
    cores = lax.axis_size("sub")
    direct = tile_count == 4
    assert map_count == 1 and pixel_count == PIX and tile_count != 8
    slots = send_pick.shape[0]
    per_pair = slots // tile_count // LOW
    groups = slots // LOW
    scal = jnp.stack([lax.axis_index(n).astype(jnp.int32) for n in ("tile", "chan", "sub")])
    cyc = cycle_maps.reshape(CIN, PIX)
    cot = cotangent.reshape(CH, PIX)
    n_send = tile_count - 1 if direct else 1

    def exchange(sends):
        if direct:
            return [
                lax.ppermute(x, "tile", [(i, i ^ s) for i in range(tile_count)])
                for s, x in zip(range(1, tile_count), sends)
            ]
        return [lax.all_to_all(sends[0], "tile", 0, 0, tiled=True)]

    def sent(dims, kind):
        if direct:
            return [shape(dims, kind)] * n_send
        return [shape((tile_count,) + dims, kind)]

    if direct:
        block_shapes = [shape((CIN, per_pair, LOW), BF16)] * tile_count
    else:
        block_shapes = [shape((tile_count, CIN, per_pair, LOW), BF16)]
    call = lambda kernel, name, flops, moved, limit, **kw: pl.pallas_call(
        kernel, name=name, cost_estimate=cost(flops, moved), compiler_params=tile_params(limit), **kw
    )
    conv_flops = 2 * 9 * CH * CH * PIX
    blocks = call(
        functools.partial(send_kernel, tile_count, direct),
        "send_pick",
        2 * CIN * PIX * slots,
        12 * PIX,
        8,
        in_specs=[SMEM, VMEM, VMEM],
        out_specs=[VMEM] * len(block_shapes),
        out_shape=block_shapes,
        scratch_shapes=[
            pltpu.VMEM((CIN * PIX // LOW, LOW), F32),
            pltpu.VMEM((CIN * PIX // LOW, LOW), BF16),
            pltpu.VMEM((CIN, groups, LOW), F32),
        ],
    )(scal, cyc, send_pick.reshape(slots // SIDE, SIDE))
    if direct:
        blocks = [blocks[0]] + exchange(blocks[1:])
    else:
        blocks = exchange(blocks)

    square = (3 * CH, 3 * CH)
    rims, columns, fwd_w, back_w, w1, side_w = call(
        edge_kernel,
        "edges",
        conv_flops // 8,
        2 * CH * PIX,
        16,
        grid=(STEPS,),
        in_specs=[row_block(), whole((9, CH, CH)), whole((9, CIN, CH))],
        out_specs=[
            whole((4, CH, SIDE)),
            whole((2, CH, SIDE)),
            whole(square),
            whole(square),
            whole((CH, 96)),
            whole((4, CH, 96)),
        ],
        out_shape=[
            shape((4, CH, SIDE), BF16),
            shape((2, CH, SIDE), BF16),
            shape(square, BF16),
            shape(square, BF16),
            shape((CH, 96), BF16),
            shape((4, CH, 96), BF16),
        ],
        scratch_shapes=[pltpu.VMEM((2, CH, SIDE), F32), pltpu.VMEM((SIDE, SIDE), F32)],
    )(cot, conv_second, jnp.swapaxes(conv_first, 1, 2))

    index = recv_pick.reshape(SIDE, SIDE)
    *sends, source, strips, comb = call(
        functools.partial(strip_kernel, tile_count, direct),
        "strips",
        2 * CIN * groups * LOW * 8 * SIDE,
        10 * PIX,
        8,
        in_specs=[SMEM, SMEM, SMEM] + [VMEM] * (2 + len(blocks)),
        out_specs=[VMEM] * (n_send + 3),
        out_shape=sent((COMB, SIDE), BF16)
        + [shape((CIN * groups, LOW), BF16), shape((8, 8, SIDE), F32), shape((4, COMB, SIDE), BF16)],
        scratch_shapes=[pltpu.VMEM((CIN * groups, LOW), F32)],
    )(scal, neighbour, facing, index, rims, *blocks)
    arrived = exchange(sends)

    tiles = call(
        functools.partial(main_pick_kernel, groups),
        "recv_pick",
        2 * CIN * groups * LOW * PIX,
        2 * 8 * PIX,
        8,
        in_specs=[VMEM] * 2,
        out_specs=VMEM,
        out_shape=shape((8, PIX), F32),
    )(index, source)

    pads_shapes = [shape((4, 8, SIDE), F32), shape((4, CH, SIDE), F32), shape((4, CH, SIDE), BF16)]
    table = pltpu.VMEM((5 + tile_count, COMB, SIDE), BF16)
    if direct:
        pads, rims_in, incoming = call(
            functools.partial(near_kernel, tile_count),
            "near",
            conv_flops // 128,
            PIX,
            8,
            in_specs=[SMEM] * 3 + [VMEM] * (3 + n_send),
            out_specs=[VMEM] * 3,
            out_shape=pads_shapes,
            scratch_shapes=[table, pltpu.VMEM((4, 8, SIDE), F32), pltpu.VMEM((96, SIDE), F32)],
        )(scal, neighbour, facing, strips, comb, side_w, *arrived)
        edges_in = [incoming]
    else:
        pads, rims_in, own, sends = call(
            functools.partial(border_kernel, tile_count),
            "border",
            conv_flops // 128,
            PIX,
            8,
            in_specs=[SMEM] * 3 + [VMEM] * 4,
            out_specs=[VMEM] * 4,
            out_shape=pads_shapes + sent((CH, SIDE), BF16),
            scratch_shapes=[table, pltpu.VMEM((96, 4 * SIDE), F32)],
        )(scal, neighbour, facing, strips, comb, w1, *arrived)
        edges_in = [own] + exchange([sends])

    hidden, grad, g1, g2 = call(
        middle_kernel,
        "middle",
        2 * conv_flops,
        8 * CH * PIX,
        24,
        grid=(STEPS,),
        in_specs=[
            whole((8, PIX)),
            whole((4, 8, SIDE)),
            whole((4, CH, SIDE)),
            whole((CH, 96)),
            whole(square),
            row_block(),
            row_before(),
            row_after(),
        ],
        out_specs=[row_block(), row_block(), whole((96, CH)), whole(square)],
        out_shape=[shape((CH, PIX), BF16), shape((CH, PIX), BF16), shape((96, CH), F32), shape(square, F32)],
        scratch_shapes=[
            pltpu.VMEM((32, (SIDE + 2) * SIDE), BF16),
            pltpu.VMEM((3 * CH, (ROWS + 2) * SIDE), BF16),
            pltpu.VMEM((3 * CH, (ROWS + 2) * SIDE), F32),
            pltpu.VMEM((CH, (ROWS + 3) * SIDE), BF16),
        ],
    )(tiles, pads, rims_in, w1, back_w, cot, cot, cot)

    scale = 1.0 / math.sqrt(map_count * chans * cores * tile_count * PIX)
    fast_sum = direct and chans == 2 and cores == 2
    half = 3 * CH // 2 if fast_sum else 3 * CH
    top = pl.BlockSpec((CH, SIDE), lambda i: (0, 0))
    bottom = pl.BlockSpec((CH, SIDE), lambda i: (0, SIDE - 1))
    pads2, fringe, keep, send = call(
        functools.partial(close_kernel, tile_count, direct, scale),
        "close",
        conv_flops // 128,
        PIX,
        8,
        grid=(1,),
        in_specs=[SMEM, SMEM, SMEM, whole((2, CH, SIDE)), top, bottom]
        + [whole((96, CH)), whole(square), whole(square)]
        + [whole(x.shape) for x in edges_in],
        out_specs=[whole((2, CH, SIDE)), whole((2, CH, SIDE)), whole((half, LOW)), whole((half, LOW))],
        out_shape=[
            shape((2, CH, SIDE), BF16),
            shape((2, CH, SIDE), F32),
            shape((half, LOW), F32),
            shape((half, LOW), F32),
        ],
        scratch_shapes=[pltpu.VMEM((3 * CH, LOW), F32)]
        + ([] if direct else [pltpu.VMEM((5 + tile_count, CH, SIDE), BF16)]),
    )(scal, neighbour, facing, columns, cot, cot, g1, g2, fwd_w, *edges_in)

    anywhere = pl.BlockSpec(memory_space=pl.ANY)

    def convolve(start, count, out, after):
        more = [after] if out is None else [after, out]
        return call(
            functools.partial(output_kernel, start),
            "output",
            conv_flops * count // STEPS,
            4 * CH * PIX * count // STEPS,
            12,
            grid=(count,),
            in_specs=[
                row_block(start),
                row_before(start),
                row_after(start),
                whole((2, CH, SIDE)),
                whole((2, CH, SIDE)),
                whole(square),
            ]
            + [anywhere] * len(more),
            out_specs=[row_block(start), whole((8, SIDE))],
            out_shape=[shape((CH, PIX), BF16), shape((8, SIDE), F32)],
            input_output_aliases={} if out is None else {7: 0},
        )(hidden, hidden, hidden, pads2, fringe, fwd_w, *more)

    finals = [shape((9, CIN, CH), F32), shape((9, CH, CH), F32)]
    if fast_sum:
        swap = lambda x, name: lax.ppermute(x, name, [(0, 1), (1, 0)])
        quarter = half // 2
        small = lambda kernel, name, **kw: call(kernel, name, 1000, half * LOW * 16, 4, **kw)
        got = swap(send, "sub")
        out, token = convolve(0, 1, None, send)
        keep2, send2 = small(
            pair_kernel,
            "pair",
            in_specs=[SMEM, VMEM, VMEM, anywhere],
            out_specs=[VMEM, VMEM],
            out_shape=[shape((quarter, LOW), F32)] * 2,
            scratch_shapes=[pltpu.VMEM((half, LOW), F32)],
        )(scal, keep, got, token)
        got = swap(send2, "chan")
        out, token = convolve(1, 2, out, send2)
        got, _ = lax.optimization_barrier((got, token))
        mine = keep2 + got
        got = exchange([mine] * n_send)
        out, token = convolve(3, 3, out, mine)
        mine = small(
            functools.partial(ring_kernel, tile_count),
            "ring",
            in_specs=[SMEM] + [VMEM] * tile_count + [anywhere],
            out_specs=VMEM,
            out_shape=shape((quarter, LOW), F32),
            scratch_shapes=[pltpu.VMEM((tile_count, quarter, LOW), F32)],
        )(scal, mine, *got, token)
        got = swap(mine, "chan")
        out, token = convolve(6, 2, out, mine)
        mine = small(
            join_kernel,
            "join",
            in_specs=[SMEM, VMEM, VMEM, anywhere],
            out_specs=VMEM,
            out_shape=shape((half, LOW), F32),
        )(scal, mine, got, token)
        got = swap(mine, "sub")
        first, second = small(
            last_kernel,
            "last",
            in_specs=[SMEM, VMEM, VMEM],
            out_specs=[VMEM, VMEM],
            out_shape=finals,
            scratch_shapes=[pltpu.VMEM((3 * CH, LOW), F32)],
        )(scal, mine, got)
    else:
        out, _ = convolve(0, STEPS, None, send)
        total = lax.psum(keep, ("tile", "chan", "sub"))
        first, second = pl.pallas_call(
            unpack, in_specs=[VMEM], out_specs=[VMEM, VMEM], out_shape=finals, name="unpack"
        )(total)
    return (out.reshape(1, CH, PIX), grad.reshape(1, CH, PIX), jnp.swapaxes(first, 1, 2), second)


def solution(mesh):
    in_specs = (
        P(("groups", "chan", "sub"), None, "tile"),
        P("tile"),
        P("tile"),
        P(),
        P(),
        P(),
        P(),
        P(("groups", "chan", "sub"), None, "tile"),
    )
    out_specs = (
        P(("groups", "chan", "sub"), None, "tile"),
        P(("groups", "chan", "sub"), None, "tile"),
        P("groups", None, None),
        P("groups", None, None),
    )
    return jax.shard_map(body, mesh=mesh, in_specs=in_specs, out_specs=out_specs, check_vma=False)
```

```python
import functools
import math

import jax
import jax.numpy as jnp
from jax import lax
from jax.experimental import pallas as pl
from jax.experimental.pallas import tpu as pltpu
from jax.sharding import PartitionSpec as P

SIDE = 128
PIX = SIDE * SIDE
CH = 64
CIN = 3
LOW = 256
COMB = 96
ROWS = 32
STEPS = SIDE // ROWS
F32 = jnp.float32
BF16 = jnp.bfloat16
SMEM = pl.BlockSpec(memory_space=pltpu.SMEM)
VMEM = pl.BlockSpec(memory_space=pltpu.VMEM)


def iota(shape, dim):
    return lax.broadcasted_iota(jnp.int32, shape, dim)


def hot(a, b):
    return jnp.where(a == b, 1.0, 0.0).astype(BF16)


def dot(a, b):
    return jnp.dot(a, b, preferred_element_type=F32)


def dot_nt(a, b):
    return lax.dot_general(a, b, (((1,), (1,)), ((), ())), preferred_element_type=F32)


def reverse(strip):
    swap = hot(iota((SIDE, SIDE), 0) + iota((SIDE, SIDE), 1), SIDE - 1)
    return dot(strip.astype(BF16), swap)


def from_left(x):
    return jnp.where(iota(x.shape, 1) == 0, 0.0, pltpu.roll(x, 1, 1))


def from_right(x):
    return jnp.where(iota(x.shape, 1) == SIDE - 1, 0.0, pltpu.roll(x, SIDE - 1, 1))


def keep_lane(lane):
    return jnp.where(iota((CH, SIDE), 1) == lane, 0.0, 1.0).astype(BF16)


def ends_table(shift, east):
    src = iota((SIDE, 2 * SIDE), 0)
    lane = iota((SIDE, 2 * SIDE), 1)
    return hot(lane, 2 * (src - shift) + (0 if east else 1))


def row_ends(pairs, row):
    half = row // (SIDE // 2)
    back = lax.rem(4 * SIDE - 2 * row - 1, SIDE)
    return pltpu.roll(pairs[half], back, 1)


def is_end(shape):
    lane = iota(shape, 1)
    return (lane == 0) | (lane == SIDE - 1)


def pick_rows(low_rows, high_rows, groups, source):
    low = jnp.broadcast_to(low_rows, (LOW, LOW)).astype(jnp.int16)
    rows = iota((LOW, LOW), 0).astype(jnp.int16)
    found = dot(source, jnp.where(low == rows, jnp.bfloat16(1), jnp.bfloat16(0)))
    lines = iota((8, LOW), 0)
    accs = [jnp.zeros((8, LOW), F32)] * CIN
    for g in range(groups // 8):
        here = lines == high_rows - 8 * g
        for c in range(CIN):
            at = c * groups + 8 * g
            accs[c] = jnp.where(here, found[at : at + 8], accs[c])
    return [jnp.sum(x, axis=0, keepdims=True) for x in accs]


def split_index(index):
    return index & (LOW - 1), index >> 8


def tile_params(limit_mib):
    return pltpu.CompilerParams(vmem_limit_bytes=limit_mib << 20)


def send_kernel(tile_count, direct, scal, cyc, index, *rest):
    outs, (stage, source, found) = rest[:-3], rest[-3:]
    groups = PIX // LOW
    per_dest = index.shape[0] // 2 // tile_count
    whole = cyc[...].astype(F32)
    for h in range(groups):
        piece = whole[:, h * LOW : (h + 1) * LOW]
        for c in range(CIN):
            stage[pl.ds(c * groups + h, 1), :] = piece[c : c + 1]
    source[...] = stage[...].astype(BF16)
    data = source[...]
    me = scal[0]

    def chunk(m, carry):
        if direct:
            dest = me ^ (m // per_dest)
            at = dest * per_dest + lax.rem(m, per_dest)
        else:
            at = m
        row = jnp.concatenate([index[pl.ds(2 * at, 1), :], index[pl.ds(2 * at + 1, 1), :]], axis=1)
        low, high = split_index(row)
        picked = pick_rows(low, high, groups, data)
        for c in range(CIN):
            found[c, pl.ds(m, 1), :] = picked[c]
        return carry

    lax.fori_loop(0, tile_count * per_dest, chunk, 0, unroll=32)
    for d in range(tile_count):
        for c in range(CIN):
            block = found[c, d * per_dest : (d + 1) * per_dest, :].astype(BF16)
            if direct:
                outs[d][c] = block
            else:
                outs[0][d, c] = block


def side_towards(nbr, me, dest):
    side = jnp.int32(0)
    for k in range(4):
        side = jnp.where(nbr[me, k] == dest, k, side)
    return side


def send_strips(tile_count, direct, nbr, me, strips, outs):
    if direct:
        for s in range(1, tile_count):
            dest = me ^ s
            outs[s - 1][...] = strips[side_towards(nbr, me, dest)]
    else:
        for dest in range(tile_count):
            outs[0][dest] = strips[side_towards(nbr, me, dest)]


def take_strips(tile_count, direct, nbr, fac, me, own, arrived, table):
    for k in range(4):
        table[k] = own[k]
    if direct:
        for s in range(1, tile_count):
            table[4 + (me ^ s)] = arrived[s - 1][...]
    else:
        for d in range(tile_count):
            table[4 + d] = arrived[0][d]
    table[4 + tile_count] = jnp.zeros(table.shape[1:], table.dtype)
    got = []
    for k in range(4):
        other = nbr[me, k]
        at = jnp.where(other == me, fac[me, k], 4 + other)
        at = jnp.where(other < 0, 4 + tile_count, at)
        got.append(table[at])
    return got


def side_ends(north, east, south, west):
    at = lambda x, i: x[:, i : i + 1]
    last = SIDE - 1
    fours = [
        (at(west, 0), at(east, 0), at(west, 1), at(east, 1)),
        (at(north, last), at(south, last), at(north, last - 1), at(south, last - 1)),
        (at(east, last), at(west, last), at(east, last - 1), at(west, last - 1)),
        (at(south, 0), at(north, 0), at(south, 1), at(north, 1)),
    ]
    lane = iota((8, SIDE), 1)
    lines = []
    for four in fours:
        line = jnp.zeros((8, SIDE), F32)
        for n, value in enumerate(four):
            line = jnp.where(lane == n, value, line)
        lines.append(line)
    return lines


def strip_kernel(tile_count, direct, scal, nbr, fac, index, rims, *rest):
    n_in = tile_count if direct else 1
    n_out = tile_count - 1 if direct else 1
    blocks, rest = rest[:n_in], rest[n_in:]
    sends, rest = rest[:n_out], rest[n_out:]
    source, strips, comb, stage = rest
    me = scal[0]
    per_src = blocks[0].shape[-2]
    groups = tile_count * per_src
    for s in range(tile_count):
        for c in range(CIN):
            if direct:
                src = me ^ s
                at = c * groups + src * per_src
                if per_src % 8 == 0:
                    at = pl.multiple_of(at, 8)
                stage[pl.ds(at, per_src), :] = blocks[s][c].astype(F32)
            else:
                at = c * groups + s * per_src
                stage[at : at + per_src, :] = blocks[0][s, c].astype(F32)
    source[...] = stage[...].astype(BF16)
    data = source[...]
    flipped = index[...].astype(F32).T
    col = lambda j: flipped[j : j + 1, :].astype(jnp.int32)
    row = lambda i: index[i : i + 1, :]
    pairs = [(row(0), row(1)), (row(126), row(127)), (col(0), col(1)), (col(126), col(127))]
    for n, pair in enumerate(pairs):
        low, high = split_index(jnp.concatenate(pair, axis=1))
        picked = pick_rows(low, high, groups, data)
        for c in range(CIN):
            strips[2 * n, c : c + 1, :] = picked[c][:, :SIDE]
            strips[2 * n + 1, c : c + 1, :] = picked[c][:, SIDE:]
    for n in range(8):
        strips[n, CIN:, :] = jnp.zeros((8 - CIN, SIDE), F32)
    edge = [strips[0], strips[7], reverse(strips[3]), reverse(strips[4])]
    inner = [strips[1], strips[6], reverse(strips[2]), reverse(strips[5])]
    blank = jnp.zeros((COMB - CH - 16, SIDE), F32)
    for k in range(4):
        comb[k, :CH, :] = rims[k]
        comb[k, CH:, :] = jnp.concatenate([edge[k], inner[k], blank], axis=0).astype(BF16)
    if direct:
        pads = []
        for k in range(4):
            mine = comb[jnp.where(nbr[me, k] == me, fac[me, k], 0), CH : CH + 16, :].astype(F32)[:8]
            mine = jnp.where(nbr[me, k] == me, mine, 0.0)
            pads.append(reverse(mine) if k < 2 else mine)
        blank = jnp.zeros((8, SIDE), F32)
        for k, line in enumerate(side_ends(*pads)):
            comb[k, CH + 16 :, :] = jnp.concatenate([line, blank], axis=0).astype(BF16)
    send_strips(tile_count, direct, nbr, me, comb, sends)


def main_pick_kernel(groups, index, source, out):
    data = source[...]

    def chunk(m, carry):
        row = jnp.concatenate([index[pl.ds(2 * m, 1), :], index[pl.ds(2 * m + 1, 1), :]], axis=1)
        low, high = split_index(row)
        picked = pick_rows(low, high, groups, data)
        lanes = pl.ds(pl.multiple_of(m * LOW, LOW), LOW)
        for c in range(CIN):
            out[c : c + 1, lanes] = picked[c]
        return carry

    lax.fori_loop(0, PIX // LOW, chunk, 0, unroll=32)
    out[CIN:, :] = jnp.zeros((8 - CIN, PIX), F32)


def edge_kernel(cot, conv_second, conv_first, rims, columns, fwd_w, back_w, w1, side_w, acc, table):
    step = pl.program_id(0)

    @pl.when(step == 0)
    def _():
        for a in range(3):
            for b in range(3):
                w = conv_second[3 * a + b]
                fwd_w[a * CH : (a + 1) * CH, b * CH : (b + 1) * CH] = w
                back_w[a * CH : (a + 1) * CH, b * CH : (b + 1) * CH] = w.astype(F32).T.astype(BF16)
        table[...] = jnp.zeros_like(table)
        for side in range(4):
            for t in range(3):
                for u in range(3):
                    p = [3 * t + u, 3 * u + 2 - t, 3 * (2 - t) + 2 - u, 3 * (2 - u) + t][side]
                    table[32 * t + 8 * u : 32 * t + 8 * u + CIN, :CH] = conv_first[p].astype(F32)
            side_w[side] = table[...].T[:CH, : 3 * 32].astype(BF16)
        w1[...] = side_w[0]
        acc[...] = jnp.zeros_like(acc)

    half = step // (STEPS // 2)
    got = acc[half]
    pair = iota((CH, SIDE), 1) // 2
    for t in range(ROWS):
        r = step * ROWS + t
        line = cot[:, t * SIDE : (t + 1) * SIDE].astype(F32)
        turned = pltpu.roll(line, lax.rem(2 * r + 1, SIDE), 1)
        got = jnp.where(pair == lax.rem(r, SIDE // 2), turned, got)
    acc[half] = got

    def rim_row(line, a):
        line = line.astype(F32)
        three = jnp.concatenate([from_right(line), line, from_left(line)], axis=0).astype(BF16)
        return dot(back_w[a * CH : (a + 1) * CH, :], three)

    @pl.when(step == 0)
    def _():
        rims[0] = rim_row(cot[:, :SIDE], 0).astype(BF16)

    @pl.when(step == STEPS - 1)
    def _():
        rims[2] = reverse(rim_row(cot[:, (ROWS - 1) * SIDE :], 2)).astype(BF16)
        k = iota((2 * SIDE, 2 * SIDE), 0)
        n = iota((2 * SIDE, 2 * SIDE), 1)
        sort = hot(k, jnp.where(n < SIDE, 2 * n + 1, 2 * (n - SIDE)))
        both = jnp.concatenate([acc[0], acc[1]], axis=1).astype(BF16)
        both = dot(both, sort)
        for e in range(2):
            line = both[:, e * SIDE : (e + 1) * SIDE]
            columns[e] = line.astype(BF16)
            rim = jnp.zeros((CH, SIDE), F32)
            for a, near in enumerate((from_right(line), line, from_left(line))):
                w = back_w[a * CH : (a + 1) * CH, 2 * e * CH : (2 * e + 1) * CH]
                rim = rim + dot(w, near.astype(BF16))
            if e == 0:
                rims[3] = reverse(rim).astype(BF16)
            else:
                rims[1] = rim.astype(BF16)


def shifted(line, first, last):
    lane = iota(line.shape, 1)
    left = jnp.where(lane == 0, first, pltpu.roll(line, 1, 1))
    right = jnp.where(lane == SIDE - 1, last, pltpu.roll(line, SIDE - 1, 1))
    return [left, line, right]


def deliver(got, pads, rims_in, rims_cols):
    north = [reverse(got[0]), reverse(got[1]), got[2].astype(F32), got[3].astype(F32)]
    pad = [x[CH : CH + 8] for x in north]
    rims_in[0] = north[0][:CH]
    rims_in[1] = north[2][:CH]
    cols = dot(north[3][:CH].astype(BF16), ends_table(0, False))
    cols = cols + dot(north[1][:CH].astype(BF16), ends_table(0, True))
    rims_cols[0] = cols[:, :SIDE].astype(BF16)
    rims_cols[1] = cols[:, SIDE:].astype(BF16)
    pads[0] = pad[0]
    pads[1] = pad[2]
    cols = dot(pad[3].astype(BF16), ends_table(0, False)) + dot(pad[1].astype(BF16), ends_table(0, True))
    pads[2] = cols[:, :SIDE]
    pads[3] = cols[:, SIDE:]
    return pad


def near_kernel(tile_count, scal, nbr, fac, strips, comb, side_w, *rest):
    n = tile_count - 1
    arrived, (pads, rims_in, rims_cols, incoming, table, ends, lines) = rest[:n], rest[n:]
    me = scal[0]
    got = take_strips(tile_count, True, nbr, fac, me, comb, arrived, table)
    pad = deliver(got, pads, rims_in, rims_cols)
    for k, line in enumerate(side_ends(*pad)):
        ends[k] = line
    lines[...] = jnp.zeros_like(lines)
    zero = jnp.zeros((8, 1), F32)
    for k in range(4):
        other, face = nbr[me, k], fac[me, k]
        there = got[k][CH:].astype(F32)
        end = jnp.where(other == me, ends[face], there[16:24])
        at = lambda i: end[:, i : i + 1]
        outer = reverse(comb[k, CH : CH + 16, :])[:8]
        three = [(outer, zero, zero), (there[:8], at(0), at(1)), (there[8:16], at(2), at(3))]
        for t, line in enumerate(three):
            for u, value in enumerate(shifted(*line)):
                lines[32 * t + 8 * u : 32 * t + 8 * u + 8, :] = value
        pre = dot(side_w[face], lines[...].astype(BF16))
        hid = jnp.where(other < 0, 0.0, pre * jax.nn.sigmoid(pre))
        incoming[k] = (reverse(hid) if k < 2 else hid).astype(BF16)


def border_kernel(tile_count, scal, nbr, fac, strips, comb, w1_ref, arrived, *rest):
    pads, rims_in, rims_cols, own, sends, table, lines = rest
    me = scal[0]
    w1 = w1_ref[...]
    got = take_strips(tile_count, False, nbr, fac, me, comb, [arrived], table)
    pad = deliver(got, pads, rims_in, rims_cols)
    zero = jnp.zeros((8, 1), F32)
    at = lambda x, i: x[:, i : i + 1]
    n0, e0, s0, w0 = pad
    st = [strips[i] for i in range(8)]
    across = [
        (0, [(n0, zero, zero), (st[0], at(w0, 0), at(e0, 0)), (st[1], at(w0, 1), at(e0, 1))]),
        (2, [(st[2], at(w0, 126), at(e0, 126)), (st[3], at(w0, 127), at(e0, 127)), (s0, zero, zero)]),
    ]
    along = [
        (3, [(w0, zero, zero), (st[4], at(n0, 0), at(s0, 0)), (st[5], at(n0, 1), at(s0, 1))]),
        (1, [(st[6], at(n0, 126), at(s0, 126)), (st[7], at(n0, 127), at(s0, 127)), (e0, zero, zero)]),
    ]
    lines[...] = jnp.zeros_like(lines)
    for side, three in across:
        for a, line in enumerate(three):
            for b, value in enumerate(shifted(*line)):
                lines[32 * a + 8 * b : 32 * a + 8 * b + 8, side * SIDE : (side + 1) * SIDE] = value
    for side, three in along:
        for b, line in enumerate(three):
            for a, value in enumerate(shifted(*line)):
                lines[32 * a + 8 * b : 32 * a + 8 * b + 8, side * SIDE : (side + 1) * SIDE] = value
    pre = dot(w1, lines[...].astype(BF16))
    hid = (pre * jax.nn.sigmoid(pre)).astype(BF16)
    side = lambda k: hid[:, k * SIDE : (k + 1) * SIDE]
    own[0] = side(0)
    own[1] = side(1)
    own[2] = reverse(side(2)).astype(BF16)
    own[3] = reverse(side(3)).astype(BF16)
    send_strips(tile_count, False, nbr, me, own, [sends])


def middle_kernel(
    tiles, pads, rims_in, rims_cols, w1_ref, back_w, cot, prev, nxt, hidden, grad, g1, g2, planes, near, kept
):
    step = pl.program_id(0)

    @pl.when(step == 0)
    def _():
        g1[...] = jnp.zeros_like(g1)
        g2[...] = jnp.zeros_like(g2)
        kept[:, : 2 * SIDE] = jnp.zeros((CH, 2 * SIDE), BF16)
        rest = jnp.zeros((8, SIDE), F32)

        def put(row, line, ends):
            three = shifted(line, ends, ends)
            planes[:, row * SIDE : (row + 1) * SIDE] = jnp.concatenate(three + [rest], axis=0).astype(BF16)

        put(0, pads[0], rest)
        put(SIDE + 1, pads[1], rest)
        for i in range(SIDE):
            back = (4 * SIDE - 2 * i - 1) % SIDE
            ends = pltpu.roll(pads[2 + i // (SIDE // 2)], back, 1)
            put(i + 1, tiles[:, i * SIDE : (i + 1) * SIDE], ends)

    w1 = w1_ref[...]
    weights = back_w[...]
    no_first, no_last = keep_lane(0), keep_lane(SIDE - 1)
    end = is_end((CH, SIDE))

    def weigh(first, count):
        three = [kept[:, (first + a) * SIDE : (first + a + count) * SIDE] for a in range(3)]
        return dot_nt(near[:, first * SIDE : (first + count) * SIDE], jnp.concatenate(three, axis=0))

    open_sum = open_last = None
    slopes = []
    for p in range(ROWS // 2 + 1):
        for t in (2 * p, 2 * p + 1):
            if t == 0:
                line = jnp.where(step > 0, prev[...], jnp.zeros_like(prev))
            elif t == ROWS + 1:
                line = jnp.where(step < STEPS - 1, nxt[...], jnp.zeros_like(nxt))
            else:
                line = cot[:, (t - 1) * SIDE : t * SIDE]
            lanes = slice(t * SIDE, (t + 1) * SIDE)
            near[:CH, lanes] = pltpu.roll(line, SIDE - 1, 1) * no_last
            near[CH : 2 * CH, lanes] = line
            near[2 * CH :, lanes] = pltpu.roll(line, 1, 1) * no_first
        z = dot(weights, near[:, 2 * p * SIDE : (2 * p + 2) * SIDE])
        part = lambda a, r: z[a * CH : (a + 1) * CH, r * SIDE : (r + 1) * SIDE]
        if p > 0:
            pair = [open_sum + part(0, 0), part(0, 1) + part(1, 0) + open_last]
            base = step * ROWS + 2 * p - 2
            cols = []
            for a in range(3):
                lanes = pl.ds(pl.multiple_of((base + a) * SIDE, SIDE), 2 * SIDE)
                cols.append(planes[:, lanes])
            pre = dot(w1, jnp.concatenate(cols, axis=0))
            sigma = jax.nn.sigmoid(pre)
            hid = pre * sigma
            slope = sigma + hid * (1.0 - sigma)
            for r in range(2):
                t = 2 * p - 2 + r
                line = pair[r]
                line = line + jnp.where(end, row_ends(rims_cols, base + r).astype(F32), 0.0)
                if t == 0:
                    line = line + jnp.where(step == 0, rims_in[0], 0.0)
                if t == ROWS - 1:
                    line = line + jnp.where(step == STEPS - 1, rims_in[1], 0.0)
                grad[:, t * SIDE : (t + 1) * SIDE] = line.astype(BF16)
                slopes.append((line * slope[:, r * SIDE : (r + 1) * SIDE]).astype(BF16))
            hid = hid.astype(BF16)
            hidden[:, (2 * p - 2) * SIDE : 2 * p * SIDE] = hid
            kept[:, 2 * p * SIDE : (2 * p + 2) * SIDE] = hid
        open_sum = part(1, 1) + part(2, 0)
        open_last = part(2, 1)
        if p > 0 and p % 4 == 0:
            count = len(slopes)
            cols = []
            for a in range(3):
                lanes = pl.ds(pl.multiple_of((step * ROWS + 2 * p - count + a) * SIDE, SIDE), count * SIDE)
                cols.append(planes[:, lanes])
            g1[...] += dot_nt(jnp.concatenate(cols, axis=0), jnp.concatenate(slopes, axis=1))
            slopes = []
        if p > 0 and p % 8 == 0:
            g2[...] += weigh(2 * p - 16, 16)

    @pl.when(step == STEPS - 1)
    def _():
        kept[:, (ROWS + 2) * SIDE :] = jnp.zeros((CH, SIDE), BF16)
        g2[...] += weigh(ROWS, 1)

    kept[:, : 2 * SIDE] = kept[:, ROWS * SIDE : (ROWS + 2) * SIDE]


def close_kernel(tile_count, direct, scale, scal, nbr, fac, columns, top, bottom, g1, g2, *rest):
    if direct:
        incoming, pads, keep, send, total = rest
        north, east, south, west = [incoming[k] for k in range(4)]
    else:
        own, arrived, pads, keep, send, total, table = rest
        got = take_strips(tile_count, direct, nbr, fac, scal[0], own, [arrived], table)
        north, east = reverse(got[0]).astype(BF16), reverse(got[1]).astype(BF16)
        south, west = got[2], got[3]
    pads[0] = north
    pads[1] = south
    side = dot(west, ends_table(0, False)) + dot(east, ends_table(0, True))
    pads[2] = side[:, :SIDE].astype(BF16)
    pads[3] = side[:, SIDE:].astype(BF16)
    total[:, : 3 * CH] = g2[...] * scale
    total[:, 3 * CH :] = jnp.zeros((3 * CH, CH), F32)
    total[: 3 * 32, 3 * CH :] = g1[...] * scale

    def three_ways(line, turned):
        line = line.astype(F32)
        ways = [from_right(line), line, from_left(line)]
        return jnp.concatenate(ways[::-1] if turned else ways, axis=0).astype(BF16)

    total[:, :CH] += dot_nt(three_ways(top[...], False), north) * scale
    total[:, 2 * CH : 3 * CH] += dot_nt(three_ways(bottom[...], False), south) * scale
    total[:CH, : 3 * CH] += dot_nt(columns[0], three_ways(west, True)) * scale
    total[2 * CH :, : 3 * CH] += dot_nt(columns[1], three_ways(east, True)) * scale
    core = scal[2]
    half = keep.shape[0]
    if half == 3 * CH:
        keep[...] = total[...]
        send[...] = jnp.zeros_like(send)
    else:
        keep[...] = total[pl.ds(pl.multiple_of(core * half, 8), half), :]
        send[...] = total[pl.ds(pl.multiple_of((1 - core) * half, 8), half), :]


def pair_kernel(scal, kept, got, after, keep, send, total):
    total[...] = kept[...] + got[...]
    half = keep.shape[0]
    here = scal[1]
    keep[...] = total[pl.ds(pl.multiple_of(here * half, 8), half), :]
    send[...] = total[pl.ds(pl.multiple_of((1 - here) * half, 8), half), :]


def add_kernel(mine, got, after, out):
    out[...] = mine[...] + got[...]


def ring_kernel(tile_count, scal, mine, *rest):
    got, (after, out, table) = rest[:-3], rest[-3:]
    me = scal[0]
    table[me] = mine[...]
    for s in range(1, tile_count):
        table[me ^ s] = got[s - 1][...]
    total = table[0]
    for t in range(1, tile_count):
        total = total + table[t]
    out[...] = total


def join_kernel(scal, mine, got, after, out):
    half = mine.shape[0]
    here = scal[1]
    out[pl.ds(pl.multiple_of(here * half, 8), half), :] = mine[...]
    out[pl.ds(pl.multiple_of((1 - here) * half, 8), half), :] = got[...]


def unpack(total, first, second):
    for a in range(3):
        for b in range(3):
            second[3 * a + b] = total[b * CH : (b + 1) * CH, a * CH : (a + 1) * CH]
            row = 32 * a + 8 * b
            first[3 * a + b] = total[row : row + CIN, 3 * CH :]


def last_kernel(scal, mine, got, first, second, total):
    half = mine.shape[0]
    here = scal[2]
    total[pl.ds(pl.multiple_of(here * half, 8), half), :] = mine[...]
    total[pl.ds(pl.multiple_of((1 - here) * half, 8), half), :] = got[...]
    unpack(total, first, second)


def output_kernel(start, hid, prev, nxt, pads, fwd_w, *rest):
    out, token, near = rest[-3:]
    token[...] = jnp.zeros_like(token)
    step = pl.program_id(0) + start
    weights = fwd_w[...]
    lane = iota((CH, SIDE), 1)
    first, last = lane == 0, lane == SIDE - 1
    none = jnp.zeros((CH, SIDE), BF16)
    open_sum = open_first = None
    for p in range(ROWS // 2 + 1):
        for t in (2 * p, 2 * p + 1):
            row = step * ROWS + t - 1
            if t == 0:
                line = jnp.where(step > 0, prev[...], pads[0])
                ends = row_ends(pads.at[2:4], jnp.maximum(row, 0))
                ends = jnp.where(step > 0, ends, none)
            elif t == ROWS + 1:
                line = jnp.where(step < STEPS - 1, nxt[...], pads[1])
                ends = row_ends(pads.at[2:4], jnp.minimum(row, SIDE - 1))
                ends = jnp.where(step < STEPS - 1, ends, none)
            else:
                line = hid[:, (t - 1) * SIDE : t * SIDE]
                ends = row_ends(pads.at[2:4], row)
            lanes = slice(t * SIDE, (t + 1) * SIDE)
            near[:CH, lanes] = jnp.where(first, ends, pltpu.roll(line, 1, 1))
            near[CH : 2 * CH, lanes] = line
            near[2 * CH :, lanes] = jnp.where(last, ends, pltpu.roll(line, SIDE - 1, 1))
        z = dot(weights, near[:, 2 * p * SIDE : (2 * p + 2) * SIDE])
        part = lambda a, r: z[a * CH : (a + 1) * CH, r * SIDE : (r + 1) * SIDE]
        if p > 0:
            lanes = slice((2 * p - 2) * SIDE, (2 * p - 1) * SIDE)
            out[:, lanes] = (open_sum + part(2, 0)).astype(BF16)
            lanes = slice((2 * p - 1) * SIDE, 2 * p * SIDE)
            out[:, lanes] = (open_first + part(1, 0) + part(2, 1)).astype(BF16)
        open_sum = part(0, 0) + part(1, 1)
        open_first = part(0, 1)


def shape(dims, kind):
    return jax.ShapeDtypeStruct(dims, kind)


def row_block(offset=0):
    return pl.BlockSpec((CH, ROWS * SIDE), lambda i: (0, i + offset))


def row_before(offset=0):
    return pl.BlockSpec((CH, SIDE), lambda i: (0, jnp.maximum((i + offset) * ROWS - 1, 0)))


def row_after(offset=0):
    return pl.BlockSpec((CH, SIDE), lambda i: (0, jnp.minimum((i + offset + 1) * ROWS, SIDE - 1)))


def cost(flops, moved):
    return pl.CostEstimate(flops=int(flops), bytes_accessed=int(moved), transcendentals=0)


def whole(dims):
    return pl.BlockSpec(dims, lambda i: (0,) * len(dims))


def body(cycle_maps, send_pick, recv_pick, neighbour, facing, conv_first, conv_second, cotangent):
    map_count, _, pixel_count = cycle_maps.shape
    tile_count = lax.axis_size("tile")
    chans = lax.axis_size("chan")
    cores = lax.axis_size("sub")
    direct = tile_count == 4
    assert map_count == 1 and pixel_count == PIX and tile_count != 8
    slots = send_pick.shape[0]
    per_pair = slots // tile_count // LOW
    groups = slots // LOW
    scal = jnp.stack([lax.axis_index(n).astype(jnp.int32) for n in ("tile", "chan", "sub")])
    cyc = cycle_maps.reshape(CIN, PIX)
    cot = cotangent.reshape(CH, PIX)
    n_send = tile_count - 1 if direct else 1

    def exchange(sends):
        if direct:
            return [
                lax.ppermute(x, "tile", [(i, i ^ s) for i in range(tile_count)])
                for s, x in zip(range(1, tile_count), sends)
            ]
        return [lax.all_to_all(sends[0], "tile", 0, 0, tiled=True)]

    def sent(dims, kind):
        if direct:
            return [shape(dims, kind)] * n_send
        return [shape((tile_count,) + dims, kind)]

    if direct:
        block_shapes = [shape((CIN, per_pair, LOW), BF16)] * tile_count
    else:
        block_shapes = [shape((tile_count, CIN, per_pair, LOW), BF16)]
    call = lambda kernel, name, flops, moved, limit, **kw: pl.pallas_call(
        kernel, name=name, cost_estimate=cost(flops, moved), compiler_params=tile_params(limit), **kw
    )
    conv_flops = 2 * 9 * CH * CH * PIX
    blocks = call(
        functools.partial(send_kernel, tile_count, direct),
        "send_pick",
        2 * CIN * PIX * slots,
        12 * PIX,
        8,
        in_specs=[SMEM, VMEM, VMEM],
        out_specs=[VMEM] * len(block_shapes),
        out_shape=block_shapes,
        scratch_shapes=[
            pltpu.VMEM((CIN * PIX // LOW, LOW), F32),
            pltpu.VMEM((CIN * PIX // LOW, LOW), BF16),
            pltpu.VMEM((CIN, groups, LOW), F32),
        ],
    )(scal, cyc, send_pick.reshape(slots // SIDE, SIDE))
    if direct:
        blocks = [blocks[0]] + exchange(blocks[1:])
    else:
        blocks = exchange(blocks)

    square = (3 * CH, 3 * CH)
    rims, columns, fwd_w, back_w, w1, side_w = call(
        edge_kernel,
        "edges",
        conv_flops // 8,
        2 * CH * PIX,
        16,
        grid=(STEPS,),
        in_specs=[row_block(), whole((9, CH, CH)), whole((9, CIN, CH))],
        out_specs=[
            whole((4, CH, SIDE)),
            whole((2, CH, SIDE)),
            whole(square),
            whole(square),
            whole((CH, 96)),
            whole((4, CH, 96)),
        ],
        out_shape=[
            shape((4, CH, SIDE), BF16),
            shape((2, CH, SIDE), BF16),
            shape(square, BF16),
            shape(square, BF16),
            shape((CH, 96), BF16),
            shape((4, CH, 96), BF16),
        ],
        scratch_shapes=[pltpu.VMEM((2, CH, SIDE), F32), pltpu.VMEM((SIDE, SIDE), F32)],
    )(cot, conv_second, jnp.swapaxes(conv_first, 1, 2))

    index = recv_pick.reshape(SIDE, SIDE)
    *sends, source, strips, comb = call(
        functools.partial(strip_kernel, tile_count, direct),
        "strips",
        2 * CIN * groups * LOW * 8 * SIDE,
        10 * PIX,
        8,
        in_specs=[SMEM, SMEM, SMEM] + [VMEM] * (2 + len(blocks)),
        out_specs=[VMEM] * (n_send + 3),
        out_shape=sent((COMB, SIDE), BF16)
        + [shape((CIN * groups, LOW), BF16), shape((8, 8, SIDE), F32), shape((4, COMB, SIDE), BF16)],
        scratch_shapes=[pltpu.VMEM((CIN * groups, LOW), F32)],
    )(scal, neighbour, facing, index, rims, *blocks)
    arrived = exchange(sends)

    tiles = call(
        functools.partial(main_pick_kernel, groups),
        "recv_pick",
        2 * CIN * groups * LOW * PIX,
        2 * 8 * PIX,
        8,
        in_specs=[VMEM] * 2,
        out_specs=VMEM,
        out_shape=shape((8, PIX), F32),
    )(index, source)

    pads_shapes = [
        shape((4, 8, SIDE), F32),
        shape((2, CH, SIDE), F32),
        shape((2, CH, SIDE), BF16),
        shape((4, CH, SIDE), BF16),
    ]
    table = pltpu.VMEM((5 + tile_count, COMB, SIDE), BF16)
    if direct:
        pads, rims_in, rims_cols, incoming = call(
            functools.partial(near_kernel, tile_count),
            "near",
            conv_flops // 128,
            PIX,
            8,
            in_specs=[SMEM] * 3 + [VMEM] * (3 + n_send),
            out_specs=[VMEM] * 4,
            out_shape=pads_shapes,
            scratch_shapes=[table, pltpu.VMEM((4, 8, SIDE), F32), pltpu.VMEM((96, SIDE), F32)],
        )(scal, neighbour, facing, strips, comb, side_w, *arrived)
        edges_in = [incoming]
    else:
        pads, rims_in, rims_cols, own, sends = call(
            functools.partial(border_kernel, tile_count),
            "border",
            conv_flops // 128,
            PIX,
            8,
            in_specs=[SMEM] * 3 + [VMEM] * 4,
            out_specs=[VMEM] * 5,
            out_shape=pads_shapes + sent((CH, SIDE), BF16),
            scratch_shapes=[table, pltpu.VMEM((96, 4 * SIDE), F32)],
        )(scal, neighbour, facing, strips, comb, w1, *arrived)
        edges_in = [own] + exchange([sends])

    hidden, grad, g1, g2 = call(
        middle_kernel,
        "middle",
        2 * conv_flops,
        8 * CH * PIX,
        24,
        grid=(STEPS,),
        in_specs=[
            whole((8, PIX)),
            whole((4, 8, SIDE)),
            whole((2, CH, SIDE)),
            whole((2, CH, SIDE)),
            whole((CH, 96)),
            whole(square),
            row_block(),
            row_before(),
            row_after(),
        ],
        out_specs=[row_block(), row_block(), whole((96, CH)), whole(square)],
        out_shape=[shape((CH, PIX), BF16), shape((CH, PIX), BF16), shape((96, CH), F32), shape(square, F32)],
        scratch_shapes=[
            pltpu.VMEM((32, (SIDE + 2) * SIDE), BF16),
            pltpu.VMEM((3 * CH, (ROWS + 2) * SIDE), BF16),
            pltpu.VMEM((CH, (ROWS + 3) * SIDE), BF16),
        ],
    )(tiles, pads, rims_in, rims_cols, w1, back_w, cot, cot, cot)

    scale = 1.0 / math.sqrt(map_count * chans * cores * tile_count * PIX)
    fast_sum = direct and chans == 2 and cores == 2
    half = 3 * CH // 2 if fast_sum else 3 * CH
    top = pl.BlockSpec((CH, SIDE), lambda i: (0, 0))
    bottom = pl.BlockSpec((CH, SIDE), lambda i: (0, SIDE - 1))
    pads2, keep, send = call(
        functools.partial(close_kernel, tile_count, direct, scale),
        "close",
        conv_flops // 128,
        PIX,
        8,
        grid=(1,),
        in_specs=[SMEM, SMEM, SMEM, whole((2, CH, SIDE)), top, bottom]
        + [whole((96, CH)), whole(square)]
        + [whole(x.shape) for x in edges_in],
        out_specs=[whole((4, CH, SIDE)), whole((half, LOW)), whole((half, LOW))],
        out_shape=[
            shape((4, CH, SIDE), BF16),
            shape((half, LOW), F32),
            shape((half, LOW), F32),
        ],
        scratch_shapes=[pltpu.VMEM((3 * CH, LOW), F32)]
        + ([] if direct else [pltpu.VMEM((5 + tile_count, CH, SIDE), BF16)]),
    )(scal, neighbour, facing, columns, cot, cot, g1, g2, *edges_in)

    anywhere = pl.BlockSpec(memory_space=pl.ANY)

    def convolve(start, count, out, after):
        more = [after] if out is None else [after, out]
        return call(
            functools.partial(output_kernel, start),
            "output",
            conv_flops * count // STEPS,
            4 * CH * PIX * count // STEPS,
            12,
            grid=(count,),
            in_specs=[row_block(start), row_before(start), row_after(start), whole((4, CH, SIDE)), whole(square)]
            + [anywhere] * len(more),
            out_specs=[row_block(start), whole((8, SIDE))],
            out_shape=[shape((CH, PIX), BF16), shape((8, SIDE), F32)],
            input_output_aliases={} if out is None else {6: 0},
            scratch_shapes=[pltpu.VMEM((3 * CH, (ROWS + 2) * SIDE), BF16)],
        )(hidden, hidden, hidden, pads2, fwd_w, *more)

    finals = [shape((9, CIN, CH), F32), shape((9, CH, CH), F32)]
    if fast_sum:
        swap = lambda x, name: lax.ppermute(x, name, [(0, 1), (1, 0)])
        quarter = half // 2
        small = lambda kernel, name, **kw: call(kernel, name, 1000, half * LOW * 16, 4, **kw)
        got = swap(send, "sub")
        out, token = convolve(0, 1, None, send)
        keep2, send2 = small(
            pair_kernel,
            "pair",
            in_specs=[SMEM, VMEM, VMEM, anywhere],
            out_specs=[VMEM, VMEM],
            out_shape=[shape((quarter, LOW), F32)] * 2,
            scratch_shapes=[pltpu.VMEM((half, LOW), F32)],
        )(scal, keep, got, token)
        got = swap(send2, "chan")
        out, token = convolve(1, 1, out, send2)
        mine = small(
            add_kernel,
            "add",
            in_specs=[VMEM, VMEM, anywhere],
            out_specs=VMEM,
            out_shape=shape((quarter, LOW), F32),
        )(keep2, got, token)
        got = exchange([mine] * n_send)
        out, token = convolve(2, 1, out, mine)
        mine = small(
            functools.partial(ring_kernel, tile_count),
            "ring",
            in_specs=[SMEM] + [VMEM] * tile_count + [anywhere],
            out_specs=VMEM,
            out_shape=shape((quarter, LOW), F32),
            scratch_shapes=[pltpu.VMEM((tile_count, quarter, LOW), F32)],
        )(scal, mine, *got, token)
        got = swap(mine, "chan")
        out, token = convolve(3, 1, out, mine)
        mine = small(
            join_kernel,
            "join",
            in_specs=[SMEM, VMEM, VMEM, anywhere],
            out_specs=VMEM,
            out_shape=shape((half, LOW), F32),
        )(scal, mine, got, token)
        got = swap(mine, "sub")
        first, second = small(
            last_kernel,
            "last",
            in_specs=[SMEM, VMEM, VMEM],
            out_specs=[VMEM, VMEM],
            out_shape=finals,
            scratch_shapes=[pltpu.VMEM((3 * CH, LOW), F32)],
        )(scal, mine, got)
    else:
        out, _ = convolve(0, STEPS, None, send)
        total = lax.psum(keep, ("tile", "chan", "sub"))
        first, second = pl.pallas_call(
            unpack, in_specs=[VMEM], out_specs=[VMEM, VMEM], out_shape=finals, name="unpack"
        )(total)
    return (out.reshape(1, CH, PIX), grad.reshape(1, CH, PIX), jnp.swapaxes(first, 1, 2), second)


def solution(mesh):
    in_specs = (
        P(("groups", "chan", "sub"), None, "tile"),
        P("tile"),
        P("tile"),
        P(),
        P(),
        P(),
        P(),
        P(("groups", "chan", "sub"), None, "tile"),
    )
    out_specs = (
        P(("groups", "chan", "sub"), None, "tile"),
        P(("groups", "chan", "sub"), None, "tile"),
        P("groups", None, None),
        P("groups", None, None),
    )
    return jax.shard_map(body, mesh=mesh, in_specs=in_specs, out_specs=out_specs, check_vma=False)
```

```python
import functools
import math

import jax
import jax.numpy as jnp
from jax import lax
from jax.experimental import pallas as pl
from jax.experimental.pallas import tpu as pltpu
from jax.sharding import PartitionSpec as P

SIDE = 128
PIX = SIDE * SIDE
CH = 64
CIN = 3
LOW = 256
COMB = 96
ROWS = 32
STEPS = SIDE // ROWS
F32 = jnp.float32
BF16 = jnp.bfloat16
SMEM = pl.BlockSpec(memory_space=pltpu.SMEM)
VMEM = pl.BlockSpec(memory_space=pltpu.VMEM)


def iota(shape, dim):
    return lax.broadcasted_iota(jnp.int32, shape, dim)


def hot(a, b):
    return jnp.where(a == b, 1.0, 0.0).astype(BF16)


def dot(a, b):
    return jnp.dot(a, b, preferred_element_type=F32)


def dot_nt(a, b):
    return lax.dot_general(a, b, (((1,), (1,)), ((), ())), preferred_element_type=F32)


def reverse(strip):
    swap = hot(iota((SIDE, SIDE), 0) + iota((SIDE, SIDE), 1), SIDE - 1)
    return dot(strip.astype(BF16), swap)


def from_left(x):
    return jnp.where(iota(x.shape, 1) == 0, 0.0, pltpu.roll(x, 1, 1))


def from_right(x):
    return jnp.where(iota(x.shape, 1) == SIDE - 1, 0.0, pltpu.roll(x, SIDE - 1, 1))


def keep_lane(lane):
    return jnp.where(iota((CH, SIDE), 1) == lane, 0.0, 1.0).astype(BF16)


def ends_table(shift, east):
    src = iota((SIDE, 2 * SIDE), 0)
    lane = iota((SIDE, 2 * SIDE), 1)
    return hot(lane, 2 * (src - shift) + (0 if east else 1))


def row_ends(pairs, row):
    half = row // (SIDE // 2)
    back = lax.rem(4 * SIDE - 2 * row - 1, SIDE)
    return pltpu.roll(pairs[half], back, 1)


def is_end(shape):
    lane = iota(shape, 1)
    return (lane == 0) | (lane == SIDE - 1)


def pick_rows(low_rows, high_rows, groups, source):
    low = jnp.broadcast_to(low_rows, (LOW, LOW)).astype(jnp.int16)
    rows = iota((LOW, LOW), 0).astype(jnp.int16)
    found = dot(source, jnp.where(low == rows, jnp.bfloat16(1), jnp.bfloat16(0)))
    lines = iota((8, LOW), 0)
    accs = [jnp.zeros((8, LOW), F32)] * CIN
    for g in range(groups // 8):
        here = lines == high_rows - 8 * g
        for c in range(CIN):
            at = c * groups + 8 * g
            accs[c] = jnp.where(here, found[at : at + 8], accs[c])
    return [jnp.sum(x, axis=0, keepdims=True) for x in accs]


def split_index(index):
    return index & (LOW - 1), index >> 8


def tile_params(limit_mib):
    return pltpu.CompilerParams(vmem_limit_bytes=limit_mib << 20)


def send_kernel(tile_count, direct, scal, cyc, index, *rest):
    outs, (stage, source, found) = rest[:-3], rest[-3:]
    groups = PIX // LOW
    per_dest = index.shape[0] // 2 // tile_count
    whole = cyc[...].astype(F32)
    for h in range(groups):
        piece = whole[:, h * LOW : (h + 1) * LOW]
        for c in range(CIN):
            stage[pl.ds(c * groups + h, 1), :] = piece[c : c + 1]
    source[...] = stage[...].astype(BF16)
    data = source[...]
    me = scal[0]

    def chunk(m, carry):
        if direct:
            dest = me ^ (m // per_dest)
            at = dest * per_dest + lax.rem(m, per_dest)
        else:
            at = m
        row = jnp.concatenate([index[pl.ds(2 * at, 1), :], index[pl.ds(2 * at + 1, 1), :]], axis=1)
        low, high = split_index(row)
        picked = pick_rows(low, high, groups, data)
        for c in range(CIN):
            found[c, pl.ds(m, 1), :] = picked[c]
        return carry

    lax.fori_loop(0, tile_count * per_dest, chunk, 0, unroll=32)
    for d in range(tile_count):
        for c in range(CIN):
            block = found[c, d * per_dest : (d + 1) * per_dest, :].astype(BF16)
            if direct:
                outs[d][c] = block
            else:
                outs[0][d, c] = block


def side_towards(nbr, me, dest):
    side = jnp.int32(0)
    for k in range(4):
        side = jnp.where(nbr[me, k] == dest, k, side)
    return side


def send_strips(tile_count, direct, nbr, me, strips, outs):
    if direct:
        for s in range(1, tile_count):
            dest = me ^ s
            outs[s - 1][...] = strips[side_towards(nbr, me, dest)]
    else:
        for dest in range(tile_count):
            outs[0][dest] = strips[side_towards(nbr, me, dest)]


def take_strips(tile_count, direct, nbr, fac, me, own, arrived, table):
    for k in range(4):
        table[k] = own[k]
    if direct:
        for s in range(1, tile_count):
            table[4 + (me ^ s)] = arrived[s - 1][...]
    else:
        for d in range(tile_count):
            table[4 + d] = arrived[0][d]
    table[4 + tile_count] = jnp.zeros(table.shape[1:], table.dtype)
    got = []
    for k in range(4):
        other = nbr[me, k]
        at = jnp.where(other == me, fac[me, k], 4 + other)
        at = jnp.where(other < 0, 4 + tile_count, at)
        got.append(table[at])
    return got


def side_ends(north, east, south, west):
    at = lambda x, i: x[:, i : i + 1]
    last = SIDE - 1
    fours = [
        (at(west, 0), at(east, 0), at(west, 1), at(east, 1)),
        (at(north, last), at(south, last), at(north, last - 1), at(south, last - 1)),
        (at(east, last), at(west, last), at(east, last - 1), at(west, last - 1)),
        (at(south, 0), at(north, 0), at(south, 1), at(north, 1)),
    ]
    lane = iota((8, SIDE), 1)
    lines = []
    for four in fours:
        line = jnp.zeros((8, SIDE), F32)
        for n, value in enumerate(four):
            line = jnp.where(lane == n, value, line)
        lines.append(line)
    return lines


def strip_kernel(tile_count, direct, scal, nbr, fac, index, rims, *rest):
    n_in = tile_count if direct else 1
    n_out = tile_count - 1 if direct else 1
    blocks, rest = rest[:n_in], rest[n_in:]
    sends, rest = rest[:n_out], rest[n_out:]
    source, strips, comb, stage = rest
    me = scal[0]
    per_src = blocks[0].shape[-2]
    groups = tile_count * per_src
    for s in range(tile_count):
        for c in range(CIN):
            if direct:
                src = me ^ s
                at = c * groups + src * per_src
                if per_src % 8 == 0:
                    at = pl.multiple_of(at, 8)
                stage[pl.ds(at, per_src), :] = blocks[s][c].astype(F32)
            else:
                at = c * groups + s * per_src
                stage[at : at + per_src, :] = blocks[0][s, c].astype(F32)
    source[...] = stage[...].astype(BF16)
    data = source[...]
    flipped = index[...].astype(F32).T
    col = lambda j: flipped[j : j + 1, :].astype(jnp.int32)
    row = lambda i: index[i : i + 1, :]
    pairs = [(row(0), row(1)), (row(126), row(127)), (col(0), col(1)), (col(126), col(127))]
    for n, pair in enumerate(pairs):
        low, high = split_index(jnp.concatenate(pair, axis=1))
        picked = pick_rows(low, high, groups, data)
        for c in range(CIN):
            strips[2 * n, c : c + 1, :] = picked[c][:, :SIDE]
            strips[2 * n + 1, c : c + 1, :] = picked[c][:, SIDE:]
    for n in range(8):
        strips[n, CIN:, :] = jnp.zeros((8 - CIN, SIDE), F32)
    edge = [strips[0], strips[7], reverse(strips[3]), reverse(strips[4])]
    inner = [strips[1], strips[6], reverse(strips[2]), reverse(strips[5])]
    blank = jnp.zeros((COMB - CH - 16, SIDE), F32)
    for k in range(4):
        comb[k, :CH, :] = rims[k]
        comb[k, CH:, :] = jnp.concatenate([edge[k], inner[k], blank], axis=0).astype(BF16)
    if direct:
        pads = []
        for k in range(4):
            mine = comb[jnp.where(nbr[me, k] == me, fac[me, k], 0), CH : CH + 16, :].astype(F32)[:8]
            mine = jnp.where(nbr[me, k] == me, mine, 0.0)
            pads.append(reverse(mine) if k < 2 else mine)
        blank = jnp.zeros((8, SIDE), F32)
        for k, line in enumerate(side_ends(*pads)):
            comb[k, CH + 16 :, :] = jnp.concatenate([line, blank], axis=0).astype(BF16)
    send_strips(tile_count, direct, nbr, me, comb, sends)


def main_pick_kernel(groups, index, source, out):
    data = source[...]

    def chunk(m, carry):
        row = jnp.concatenate([index[pl.ds(2 * m, 1), :], index[pl.ds(2 * m + 1, 1), :]], axis=1)
        low, high = split_index(row)
        picked = pick_rows(low, high, groups, data)
        lanes = pl.ds(pl.multiple_of(m * LOW, LOW), LOW)
        for c in range(CIN):
            out[c : c + 1, lanes] = picked[c]
        return carry

    lax.fori_loop(0, PIX // LOW, chunk, 0, unroll=32)
    out[CIN:, :] = jnp.zeros((8 - CIN, PIX), F32)


def shift_rows(near, step, cot, prev, nxt):
    no_first, no_last = keep_lane(0), keep_lane(SIDE - 1)
    for t in range(ROWS + 2):
        if t == 0:
            line = jnp.where(step > 0, prev[...], jnp.zeros_like(prev))
        elif t == ROWS + 1:
            line = jnp.where(step < STEPS - 1, nxt[...], jnp.zeros_like(nxt))
        else:
            line = cot[:, (t - 1) * SIDE : t * SIDE]
        lanes = slice(t * SIDE, (t + 1) * SIDE)
        near[:CH, lanes] = pltpu.roll(line, SIDE - 1, 1) * no_last
        near[CH : 2 * CH, lanes] = line
        near[2 * CH :, lanes] = pltpu.roll(line, 1, 1) * no_first


def edge_kernel(
    cot, prev, nxt, conv_second, conv_first, hg, rims, columns, fwd_w, w1, side_w, back_w, acc, table, near
):
    step = pl.program_id(0)

    @pl.when(step == 0)
    def _():
        for a in range(3):
            for b in range(3):
                w = conv_second[3 * a + b]
                fwd_w[a * CH : (a + 1) * CH, b * CH : (b + 1) * CH] = w
                back_w[a * CH : (a + 1) * CH, b * CH : (b + 1) * CH] = w.astype(F32).T.astype(BF16)
        table[...] = jnp.zeros_like(table)
        for side in range(4):
            for t in range(3):
                for u in range(3):
                    p = [3 * t + u, 3 * u + 2 - t, 3 * (2 - t) + 2 - u, 3 * (2 - u) + t][side]
                    table[32 * t + 8 * u : 32 * t + 8 * u + CIN, :CH] = conv_first[p].astype(F32)
            side_w[side] = table[...].T[:CH, : 3 * 32].astype(BF16)
        w1[...] = side_w[0]
        acc[...] = jnp.zeros_like(acc)

    half = step // (STEPS // 2)
    got = acc[half]
    pair = iota((CH, SIDE), 1) // 2
    for t in range(ROWS):
        r = step * ROWS + t
        line = cot[:, t * SIDE : (t + 1) * SIDE].astype(F32)
        turned = pltpu.roll(line, lax.rem(2 * r + 1, SIDE), 1)
        got = jnp.where(pair == lax.rem(r, SIDE // 2), turned, got)
    acc[half] = got

    weights = back_w[...]
    shift_rows(near, step, cot, prev, nxt)
    open_sum = open_last = None
    for p in range(ROWS // 2 + 1):
        z = dot(weights, near[:, 2 * p * SIDE : (2 * p + 2) * SIDE])
        part = lambda a, r: z[a * CH : (a + 1) * CH, r * SIDE : (r + 1) * SIDE]
        if p > 0:
            hg[:, (2 * p - 2) * SIDE : (2 * p - 1) * SIDE] = open_sum + part(0, 0)
            hg[:, (2 * p - 1) * SIDE : 2 * p * SIDE] = part(0, 1) + part(1, 0) + open_last
        open_sum = part(1, 1) + part(2, 0)
        open_last = part(2, 1)

    def rim_row(line, a):
        line = line.astype(F32)
        three = jnp.concatenate([from_right(line), line, from_left(line)], axis=0).astype(BF16)
        return dot(back_w[a * CH : (a + 1) * CH, :], three)

    @pl.when(step == 0)
    def _():
        rims[0] = rim_row(cot[:, :SIDE], 0).astype(BF16)

    @pl.when(step == STEPS - 1)
    def _():
        rims[2] = reverse(rim_row(cot[:, (ROWS - 1) * SIDE :], 2)).astype(BF16)
        k = iota((2 * SIDE, 2 * SIDE), 0)
        n = iota((2 * SIDE, 2 * SIDE), 1)
        sort = hot(k, jnp.where(n < SIDE, 2 * n + 1, 2 * (n - SIDE)))
        both = jnp.concatenate([acc[0], acc[1]], axis=1).astype(BF16)
        both = dot(both, sort)
        for e in range(2):
            line = both[:, e * SIDE : (e + 1) * SIDE]
            columns[e] = line.astype(BF16)
            rim = jnp.zeros((CH, SIDE), F32)
            for a, near in enumerate((from_right(line), line, from_left(line))):
                w = back_w[a * CH : (a + 1) * CH, 2 * e * CH : (2 * e + 1) * CH]
                rim = rim + dot(w, near.astype(BF16))
            if e == 0:
                rims[3] = reverse(rim).astype(BF16)
            else:
                rims[1] = rim.astype(BF16)


def shifted(line, first, last):
    lane = iota(line.shape, 1)
    left = jnp.where(lane == 0, first, pltpu.roll(line, 1, 1))
    right = jnp.where(lane == SIDE - 1, last, pltpu.roll(line, SIDE - 1, 1))
    return [left, line, right]


def deliver(got, pads, rims_in, rims_cols):
    north = [reverse(got[0]), reverse(got[1]), got[2].astype(F32), got[3].astype(F32)]
    pad = [x[CH : CH + 8] for x in north]
    rims_in[0] = north[0][:CH]
    rims_in[1] = north[2][:CH]
    cols = dot(north[3][:CH].astype(BF16), ends_table(0, False))
    cols = cols + dot(north[1][:CH].astype(BF16), ends_table(0, True))
    rims_cols[0] = cols[:, :SIDE].astype(BF16)
    rims_cols[1] = cols[:, SIDE:].astype(BF16)
    pads[0] = pad[0]
    pads[1] = pad[2]
    cols = dot(pad[3].astype(BF16), ends_table(0, False)) + dot(pad[1].astype(BF16), ends_table(0, True))
    pads[2] = cols[:, :SIDE]
    pads[3] = cols[:, SIDE:]
    return pad


def near_part(
    tile_count, scal, nbr, fac, strips, comb, side_w, arrived, pads, rims_in, rims_cols, incoming, table, ends, lines
):
    me = scal[0]
    got = take_strips(tile_count, True, nbr, fac, me, comb, arrived, table)
    pad = deliver(got, pads, rims_in, rims_cols)
    for k, line in enumerate(side_ends(*pad)):
        ends[k] = line
    lines[...] = jnp.zeros_like(lines)
    zero = jnp.zeros((8, 1), F32)
    for k in range(4):
        other, face = nbr[me, k], fac[me, k]
        there = got[k][CH:].astype(F32)
        end = jnp.where(other == me, ends[face], there[16:24])
        at = lambda i: end[:, i : i + 1]
        outer = reverse(comb[k, CH : CH + 16, :])[:8]
        three = [(outer, zero, zero), (there[:8], at(0), at(1)), (there[8:16], at(2), at(3))]
        for t, line in enumerate(three):
            for u, value in enumerate(shifted(*line)):
                lines[32 * t + 8 * u : 32 * t + 8 * u + 8, :] = value
        pre = dot(side_w[face], lines[...].astype(BF16))
        hid = jnp.where(other < 0, 0.0, pre * jax.nn.sigmoid(pre))
        incoming[k] = (reverse(hid) if k < 2 else hid).astype(BF16)


def border_kernel(tile_count, scal, nbr, fac, strips, comb, w1_ref, arrived, *rest):
    pads, rims_in, rims_cols, own, sends, table, lines = rest
    me = scal[0]
    w1 = w1_ref[...]
    got = take_strips(tile_count, False, nbr, fac, me, comb, [arrived], table)
    pad = deliver(got, pads, rims_in, rims_cols)
    zero = jnp.zeros((8, 1), F32)
    at = lambda x, i: x[:, i : i + 1]
    n0, e0, s0, w0 = pad
    st = [strips[i] for i in range(8)]
    across = [
        (0, [(n0, zero, zero), (st[0], at(w0, 0), at(e0, 0)), (st[1], at(w0, 1), at(e0, 1))]),
        (2, [(st[2], at(w0, 126), at(e0, 126)), (st[3], at(w0, 127), at(e0, 127)), (s0, zero, zero)]),
    ]
    along = [
        (3, [(w0, zero, zero), (st[4], at(n0, 0), at(s0, 0)), (st[5], at(n0, 1), at(s0, 1))]),
        (1, [(st[6], at(n0, 126), at(s0, 126)), (st[7], at(n0, 127), at(s0, 127)), (e0, zero, zero)]),
    ]
    lines[...] = jnp.zeros_like(lines)
    for side, three in across:
        for a, line in enumerate(three):
            for b, value in enumerate(shifted(*line)):
                lines[32 * a + 8 * b : 32 * a + 8 * b + 8, side * SIDE : (side + 1) * SIDE] = value
    for side, three in along:
        for b, line in enumerate(three):
            for a, value in enumerate(shifted(*line)):
                lines[32 * a + 8 * b : 32 * a + 8 * b + 8, side * SIDE : (side + 1) * SIDE] = value
    pre = dot(w1, lines[...].astype(BF16))
    hid = (pre * jax.nn.sigmoid(pre)).astype(BF16)
    side = lambda k: hid[:, k * SIDE : (k + 1) * SIDE]
    own[0] = side(0)
    own[1] = side(1)
    own[2] = reverse(side(2)).astype(BF16)
    own[3] = reverse(side(3)).astype(BF16)
    send_strips(tile_count, False, nbr, me, own, [sends])


def middle_step(tiles, pads, rims_in, rims_cols, w1_ref, hg, cot, prev, nxt, hidden, grad, g1, g2, planes, near, kept):
    step = pl.program_id(0)

    @pl.when(step == 0)
    def _():
        g1[...] = jnp.zeros_like(g1)
        g2[...] = jnp.zeros_like(g2)
        kept[:, : 2 * SIDE] = jnp.zeros((CH, 2 * SIDE), BF16)
        rest = jnp.zeros((8, SIDE), F32)

        def put(row, line, ends):
            three = shifted(line, ends, ends)
            planes[:, row * SIDE : (row + 1) * SIDE] = jnp.concatenate(three + [rest], axis=0).astype(BF16)

        put(0, pads[0], rest)
        put(SIDE + 1, pads[1], rest)
        for i in range(SIDE):
            back = (4 * SIDE - 2 * i - 1) % SIDE
            ends = pltpu.roll(pads[2 + i // (SIDE // 2)], back, 1)
            put(i + 1, tiles[:, i * SIDE : (i + 1) * SIDE], ends)

    w1 = w1_ref[...]
    end = is_end((CH, SIDE))

    def weigh(first, count):
        three = [kept[:, (first + a) * SIDE : (first + a + count) * SIDE] for a in range(3)]
        return dot_nt(near[:, first * SIDE : (first + count) * SIDE], jnp.concatenate(three, axis=0))

    shift_rows(near, step, cot, prev, nxt)
    n_rows = 4
    acc1 = g1[...]
    for p in range(ROWS // n_rows):
        base = step * ROWS + p * n_rows
        cols = []
        for a in range(3):
            lanes = pl.ds(pl.multiple_of((base + a) * SIDE, SIDE), n_rows * SIDE)
            cols.append(planes[:, lanes])
        cols = jnp.concatenate(cols, axis=0)
        pre = dot(w1, cols)
        sigma = jax.nn.sigmoid(pre)
        hid = pre * sigma
        slope = sigma + hid * (1.0 - sigma)
        slopes = []
        for r in range(n_rows):
            t = p * n_rows + r
            line = hg[:, t * SIDE : (t + 1) * SIDE]
            line = line + jnp.where(end, row_ends(rims_cols, base + r).astype(F32), 0.0)
            if t == 0:
                line = line + jnp.where(step == 0, rims_in[0], 0.0)
            if t == ROWS - 1:
                line = line + jnp.where(step == STEPS - 1, rims_in[1], 0.0)
            grad[:, t * SIDE : (t + 1) * SIDE] = line.astype(BF16)
            slopes.append((line * slope[:, r * SIDE : (r + 1) * SIDE]).astype(BF16))
        lanes = slice(p * n_rows * SIDE, (p + 1) * n_rows * SIDE)
        hid = hid.astype(BF16)
        hidden[:, lanes] = hid
        kept[:, (p * n_rows + 2) * SIDE : ((p + 1) * n_rows + 2) * SIDE] = hid
        acc1 = acc1 + dot_nt(cols, jnp.concatenate(slopes, axis=1))
    g1[...] = acc1
    g2[...] += weigh(0, ROWS)

    @pl.when(step == STEPS - 1)
    def _():
        kept[:, (ROWS + 2) * SIDE :] = jnp.zeros((CH, SIDE), BF16)
        g2[...] += weigh(ROWS, 1)

    kept[:, : 2 * SIDE] = kept[:, ROWS * SIDE : (ROWS + 2) * SIDE]


def middle_kernel(tile_count, scale, quarters, *refs):
    scal, nbr, fac, strips, comb, side_w, *refs = refs
    arrived, refs = refs[: tile_count - 1], refs[tile_count - 1 :]
    tiles, w1_ref, hg, cot, prev, nxt, columns, top, bottom, *refs = refs
    hidden, grad, edge_pads, *refs = refs
    parts, refs = refs[:quarters], refs[quarters:]
    pads, rims_in, rims_cols, incoming, table, ends, lines, g1, g2, planes, near, kept, total = refs
    step = pl.program_id(0)

    @pl.when(step == 0)
    def _():
        near_part(
            tile_count, scal, nbr, fac, strips, comb, side_w, arrived, pads, rims_in, rims_cols, incoming, table, ends, lines
        )

    middle_step(tiles, pads, rims_in, rims_cols, w1_ref, hg, cot, prev, nxt, hidden, grad, g1, g2, planes, near, kept)

    @pl.when(step == STEPS - 1)
    def _():
        close_part(scale, scal, [incoming[k] for k in range(4)], columns, top, bottom, g1, g2, edge_pads, parts, total)


def close_kernel(tile_count, scale, scal, nbr, fac, columns, top, bottom, g1, g2, own, arrived, pads, keep, total, table):
    got = take_strips(tile_count, False, nbr, fac, scal[0], own, [arrived], table)
    four = [reverse(got[0]).astype(BF16), reverse(got[1]).astype(BF16), got[2], got[3]]
    close_part(scale, scal, four, columns, top, bottom, g1, g2, pads, [keep], total)


def close_part(scale, scal, four, columns, top, bottom, g1, g2, pads, parts, total):
    north, east, south, west = four
    pads[0] = north
    pads[1] = south
    side = dot(west, ends_table(0, False)) + dot(east, ends_table(0, True))
    pads[2] = side[:, :SIDE].astype(BF16)
    pads[3] = side[:, SIDE:].astype(BF16)
    total[:, : 3 * CH] = g2[...] * scale
    total[:, 3 * CH :] = jnp.zeros((3 * CH, CH), F32)
    total[: 3 * 32, 3 * CH :] = g1[...] * scale

    def three_ways(line, turned):
        line = line.astype(F32)
        ways = [from_right(line), line, from_left(line)]
        return jnp.concatenate(ways[::-1] if turned else ways, axis=0).astype(BF16)

    total[:, :CH] += dot_nt(three_ways(top[...], False), north) * scale
    total[:, 2 * CH : 3 * CH] += dot_nt(three_ways(bottom[...], False), south) * scale
    total[:CH, : 3 * CH] += dot_nt(columns[0], three_ways(west, True)) * scale
    total[2 * CH :, : 3 * CH] += dot_nt(columns[1], three_ways(east, True)) * scale
    if len(parts) == 1:
        parts[0][...] = total[...]
    else:
        mine = 2 * scal[1] + scal[2]
        rows = parts[0].shape[0]
        for r, part in enumerate(parts):
            part[...] = total[pl.ds(pl.multiple_of((mine ^ r) * rows, 8), rows), :]


def add_kernel(mine, one, two, three, after, out):
    out[...] = (mine[...] + one[...]) + (two[...] + three[...])


def ring_kernel(tile_count, scal, mine, *rest):
    got, (after, out, table) = rest[:-3], rest[-3:]
    me = scal[0]
    table[me] = mine[...]
    for s in range(1, tile_count):
        table[me ^ s] = got[s - 1][...]
    total = table[0]
    for t in range(1, tile_count):
        total = total + table[t]
    out[...] = total


def unpack(total, first, second):
    for a in range(3):
        for b in range(3):
            second[3 * a + b] = total[b * CH : (b + 1) * CH, a * CH : (a + 1) * CH]
            row = 32 * a + 8 * b
            first[3 * a + b] = total[row : row + CIN, 3 * CH :]


def last_kernel(scal, mine, one, two, three, first, second, total):
    here = 2 * scal[1] + scal[2]
    rows = mine.shape[0]
    for r, part in enumerate((mine, one, two, three)):
        total[pl.ds(pl.multiple_of((here ^ r) * rows, 8), rows), :] = part[...]
    unpack(total, first, second)


def output_kernel(start, hid, prev, nxt, pads, fwd_w, *rest):
    out, token, near = rest[-3:]
    token[...] = jnp.zeros_like(token)
    step = pl.program_id(0) + start
    weights = fwd_w[...]
    lane = iota((CH, SIDE), 1)
    first, last = lane == 0, lane == SIDE - 1
    none = jnp.zeros((CH, SIDE), BF16)
    open_sum = open_first = None
    for p in range(ROWS // 2 + 1):
        for t in (2 * p, 2 * p + 1):
            row = step * ROWS + t - 1
            if t == 0:
                line = jnp.where(step > 0, prev[...], pads[0])
                ends = row_ends(pads.at[2:4], jnp.maximum(row, 0))
                ends = jnp.where(step > 0, ends, none)
            elif t == ROWS + 1:
                line = jnp.where(step < STEPS - 1, nxt[...], pads[1])
                ends = row_ends(pads.at[2:4], jnp.minimum(row, SIDE - 1))
                ends = jnp.where(step < STEPS - 1, ends, none)
            else:
                line = hid[:, (t - 1) * SIDE : t * SIDE]
                ends = row_ends(pads.at[2:4], row)
            lanes = slice(t * SIDE, (t + 1) * SIDE)
            near[:CH, lanes] = jnp.where(first, ends, pltpu.roll(line, 1, 1))
            near[CH : 2 * CH, lanes] = line
            near[2 * CH :, lanes] = jnp.where(last, ends, pltpu.roll(line, SIDE - 1, 1))
        z = dot(weights, near[:, 2 * p * SIDE : (2 * p + 2) * SIDE])
        part = lambda a, r: z[a * CH : (a + 1) * CH, r * SIDE : (r + 1) * SIDE]
        if p > 0:
            lanes = slice((2 * p - 2) * SIDE, (2 * p - 1) * SIDE)
            out[:, lanes] = (open_sum + part(2, 0)).astype(BF16)
            lanes = slice((2 * p - 1) * SIDE, 2 * p * SIDE)
            out[:, lanes] = (open_first + part(1, 0) + part(2, 1)).astype(BF16)
        open_sum = part(0, 0) + part(1, 1)
        open_first = part(0, 1)


def shape(dims, kind):
    return jax.ShapeDtypeStruct(dims, kind)


def row_block(offset=0):
    return pl.BlockSpec((CH, ROWS * SIDE), lambda i: (0, i + offset))


def row_before(offset=0):
    return pl.BlockSpec((CH, SIDE), lambda i: (0, jnp.maximum((i + offset) * ROWS - 1, 0)))


def row_after(offset=0):
    return pl.BlockSpec((CH, SIDE), lambda i: (0, jnp.minimum((i + offset + 1) * ROWS, SIDE - 1)))


def cost(flops, moved):
    return pl.CostEstimate(flops=int(flops), bytes_accessed=int(moved), transcendentals=0)


def whole(dims):
    return pl.BlockSpec(dims, lambda i: (0,) * len(dims))


def body(cycle_maps, send_pick, recv_pick, neighbour, facing, conv_first, conv_second, cotangent):
    map_count, _, pixel_count = cycle_maps.shape
    tile_count = lax.axis_size("tile")
    chans = lax.axis_size("chan")
    cores = lax.axis_size("sub")
    direct = tile_count == 4
    assert map_count == 1 and pixel_count == PIX and tile_count != 8
    slots = send_pick.shape[0]
    per_pair = slots // tile_count // LOW
    groups = slots // LOW
    scal = jnp.stack([lax.axis_index(n).astype(jnp.int32) for n in ("tile", "chan", "sub")])
    cyc = cycle_maps.reshape(CIN, PIX)
    cot = cotangent.reshape(CH, PIX)
    n_send = tile_count - 1 if direct else 1

    def exchange(sends):
        if direct:
            return [
                lax.ppermute(x, "tile", [(i, i ^ s) for i in range(tile_count)])
                for s, x in zip(range(1, tile_count), sends)
            ]
        return [lax.all_to_all(sends[0], "tile", 0, 0, tiled=True)]

    def sent(dims, kind):
        if direct:
            return [shape(dims, kind)] * n_send
        return [shape((tile_count,) + dims, kind)]

    if direct:
        block_shapes = [shape((CIN, per_pair, LOW), BF16)] * tile_count
    else:
        block_shapes = [shape((tile_count, CIN, per_pair, LOW), BF16)]
    call = lambda kernel, name, flops, moved, limit, **kw: pl.pallas_call(
        kernel, name=name, cost_estimate=cost(flops, moved), compiler_params=tile_params(limit), **kw
    )
    conv_flops = 2 * 9 * CH * CH * PIX
    blocks = call(
        functools.partial(send_kernel, tile_count, direct),
        "send_pick",
        2 * CIN * PIX * slots,
        12 * PIX,
        8,
        in_specs=[SMEM, VMEM, VMEM],
        out_specs=[VMEM] * len(block_shapes),
        out_shape=block_shapes,
        scratch_shapes=[
            pltpu.VMEM((CIN * PIX // LOW, LOW), F32),
            pltpu.VMEM((CIN * PIX // LOW, LOW), BF16),
            pltpu.VMEM((CIN, groups, LOW), F32),
        ],
    )(scal, cyc, send_pick.reshape(slots // SIDE, SIDE))
    if direct:
        blocks = [blocks[0]] + exchange(blocks[1:])
    else:
        blocks = exchange(blocks)

    square = (3 * CH, 3 * CH)
    hg, rims, columns, fwd_w, w1, side_w = call(
        edge_kernel,
        "edges",
        conv_flops,
        6 * CH * PIX,
        16,
        grid=(STEPS,),
        in_specs=[row_block(), row_before(), row_after(), whole((9, CH, CH)), whole((9, CIN, CH))],
        out_specs=[
            row_block(),
            whole((4, CH, SIDE)),
            whole((2, CH, SIDE)),
            whole(square),
            whole((CH, 96)),
            whole((4, CH, 96)),
        ],
        out_shape=[
            shape((CH, PIX), F32),
            shape((4, CH, SIDE), BF16),
            shape((2, CH, SIDE), BF16),
            shape(square, BF16),
            shape((CH, 96), BF16),
            shape((4, CH, 96), BF16),
        ],
        scratch_shapes=[
            pltpu.VMEM(square, BF16),
            pltpu.VMEM((2, CH, SIDE), F32),
            pltpu.VMEM((SIDE, SIDE), F32),
            pltpu.VMEM((3 * CH, (ROWS + 2) * SIDE), BF16),
        ],
    )(cot, cot, cot, conv_second, jnp.swapaxes(conv_first, 1, 2))

    index = recv_pick.reshape(SIDE, SIDE)
    *sends, source, strips, comb = call(
        functools.partial(strip_kernel, tile_count, direct),
        "strips",
        2 * CIN * groups * LOW * 8 * SIDE,
        10 * PIX,
        8,
        in_specs=[SMEM, SMEM, SMEM] + [VMEM] * (2 + len(blocks)),
        out_specs=[VMEM] * (n_send + 3),
        out_shape=sent((COMB, SIDE), BF16)
        + [shape((CIN * groups, LOW), BF16), shape((8, 8, SIDE), F32), shape((4, COMB, SIDE), BF16)],
        scratch_shapes=[pltpu.VMEM((CIN * groups, LOW), F32)],
    )(scal, neighbour, facing, index, rims, *blocks)
    arrived = exchange(sends)

    tiles = call(
        functools.partial(main_pick_kernel, groups),
        "recv_pick",
        2 * CIN * groups * LOW * PIX,
        2 * 8 * PIX,
        8,
        in_specs=[VMEM] * 2,
        out_specs=VMEM,
        out_shape=shape((8, PIX), F32),
    )(index, source)

    pad_buffers = [((4, 8, SIDE), F32), ((2, CH, SIDE), F32), ((2, CH, SIDE), BF16), ((4, CH, SIDE), BF16)]
    table = pltpu.VMEM((5 + tile_count, COMB, SIDE), BF16)
    scale = 1.0 / math.sqrt(map_count * chans * cores * tile_count * PIX)
    fast_sum = direct and chans == 2 and cores == 2
    quarters = 4 if fast_sum else 1
    rows = 3 * CH // quarters
    top = pl.BlockSpec((CH, SIDE), lambda i: (0, 0))
    bottom = pl.BlockSpec((CH, SIDE), lambda i: (0, SIDE - 1))
    gradients = [((96, CH), F32), (square, F32)]
    work = [
        pltpu.VMEM((32, (SIDE + 2) * SIDE), BF16),
        pltpu.VMEM((3 * CH, (ROWS + 2) * SIDE), BF16),
        pltpu.VMEM((CH, (ROWS + 3) * SIDE), BF16),
    ]
    cot_blocks = [row_block(), row_block(), row_before(), row_after()]
    if direct:
        hidden, grad, pads2, *parts = call(
            functools.partial(middle_kernel, tile_count, scale, quarters),
            "middle",
            conv_flops,
            12 * CH * PIX,
            24,
            grid=(STEPS,),
            in_specs=[SMEM] * 3
            + [whole(x.shape) for x in (strips, comb, side_w, *arrived, tiles, w1)]
            + cot_blocks
            + [whole((2, CH, SIDE)), top, bottom],
            out_specs=[row_block(), row_block(), whole((4, CH, SIDE))] + [whole((rows, LOW))] * quarters,
            out_shape=[shape((CH, PIX), BF16), shape((CH, PIX), BF16), shape((4, CH, SIDE), BF16)]
            + [shape((rows, LOW), F32)] * quarters,
            scratch_shapes=[pltpu.VMEM(*x) for x in pad_buffers]
            + [table, pltpu.VMEM((4, 8, SIDE), F32), pltpu.VMEM((96, SIDE), F32)]
            + [pltpu.VMEM(*x) for x in gradients]
            + work
            + [pltpu.VMEM((3 * CH, LOW), F32)],
        )(
            *(scal, neighbour, facing, strips, comb, side_w, *arrived),
            *(tiles, w1, hg, cot, cot, cot, columns, cot, cot),
        )
    else:
        pads, rims_in, rims_cols, own, sends = call(
            functools.partial(border_kernel, tile_count),
            "border",
            conv_flops // 128,
            PIX,
            8,
            in_specs=[SMEM] * 3 + [VMEM] * 4,
            out_specs=[VMEM] * 5,
            out_shape=[shape(*x) for x in pad_buffers] + sent((CH, SIDE), BF16),
            scratch_shapes=[table, pltpu.VMEM((96, 4 * SIDE), F32)],
        )(scal, neighbour, facing, strips, comb, w1, *arrived)
        edges_in = exchange([sends])
        hidden, grad, g1, g2 = call(
            middle_step,
            "middle",
            conv_flops,
            12 * CH * PIX,
            24,
            grid=(STEPS,),
            in_specs=[whole(x.shape) for x in (tiles, pads, rims_in, rims_cols, w1)] + cot_blocks,
            out_specs=[row_block(), row_block()] + [whole(x[0]) for x in gradients],
            out_shape=[shape((CH, PIX), BF16), shape((CH, PIX), BF16)] + [shape(*x) for x in gradients],
            scratch_shapes=work,
        )(tiles, pads, rims_in, rims_cols, w1, hg, cot, cot, cot)
        pads2, *parts = call(
            functools.partial(close_kernel, tile_count, scale),
            "close",
            conv_flops // 128,
            PIX,
            8,
            grid=(1,),
            in_specs=[SMEM, SMEM, SMEM, whole((2, CH, SIDE)), top, bottom]
            + [whole(x.shape) for x in (g1, g2, own, *edges_in)],
            out_specs=[whole((4, CH, SIDE)), whole((rows, LOW))],
            out_shape=[shape((4, CH, SIDE), BF16), shape((rows, LOW), F32)],
            scratch_shapes=[pltpu.VMEM((3 * CH, LOW), F32), pltpu.VMEM((5 + tile_count, CH, SIDE), BF16)],
        )(scal, neighbour, facing, columns, cot, cot, g1, g2, own, *edges_in)

    anywhere = pl.BlockSpec(memory_space=pl.ANY)

    def convolve(start, count, out, after):
        more = [after] if out is None else [after, out]
        return call(
            functools.partial(output_kernel, start),
            "output",
            conv_flops * count // STEPS,
            4 * CH * PIX * count // STEPS,
            12,
            grid=(count,),
            in_specs=[row_block(start), row_before(start), row_after(start), whole((4, CH, SIDE)), whole(square)]
            + [anywhere] * len(more),
            out_specs=[row_block(start), whole((8, SIDE))],
            out_shape=[shape((CH, PIX), BF16), shape((8, SIDE), F32)],
            input_output_aliases={} if out is None else {6: 0},
            scratch_shapes=[pltpu.VMEM((3 * CH, (ROWS + 2) * SIDE), BF16)],
        )(hidden, hidden, hidden, pads2, fwd_w, *more)

    finals = [shape((9, CIN, CH), F32), shape((9, CH, CH), F32)]
    if fast_sum:
        group = ("chan", "sub")

        def swap(x, r):
            return lax.ppermute(x, group, [(i, i ^ r) for i in range(4)])

        small = lambda kernel, name, **kw: call(kernel, name, 1000, 4 * rows * LOW * 16, 4, **kw)
        got = [swap(parts[r], r) for r in (1, 2, 3)]
        out, token = convolve(0, 2, None, parts[1])
        mine = small(
            add_kernel,
            "add",
            in_specs=[VMEM] * 4 + [anywhere],
            out_specs=VMEM,
            out_shape=shape((rows, LOW), F32),
        )(parts[0], *got, token)
        got = exchange([mine] * n_send)
        out, token = convolve(2, 1, out, mine)
        mine = small(
            functools.partial(ring_kernel, tile_count),
            "ring",
            in_specs=[SMEM] + [VMEM] * tile_count + [anywhere],
            out_specs=VMEM,
            out_shape=shape((rows, LOW), F32),
            scratch_shapes=[pltpu.VMEM((tile_count, rows, LOW), F32)],
        )(scal, mine, *got, token)
        got = [swap(mine, r) for r in (1, 2, 3)]
        out, token = convolve(3, 1, out, mine)
        first, second = small(
            last_kernel,
            "last",
            in_specs=[SMEM] + [VMEM] * 4,
            out_specs=[VMEM, VMEM],
            out_shape=finals,
            scratch_shapes=[pltpu.VMEM((3 * CH, LOW), F32)],
        )(scal, mine, *got)
    else:
        out, _ = convolve(0, STEPS, None, parts[0])
        total = lax.psum(parts[0], ("tile", "chan", "sub"))
        first, second = pl.pallas_call(
            unpack, in_specs=[VMEM], out_specs=[VMEM, VMEM], out_shape=finals, name="unpack"
        )(total)
    return (out.reshape(1, CH, PIX), grad.reshape(1, CH, PIX), jnp.swapaxes(first, 1, 2), second)


def solution(mesh):
    in_specs = (
        P(("groups", "chan", "sub"), None, "tile"),
        P("tile"),
        P("tile"),
        P(),
        P(),
        P(),
        P(),
        P(("groups", "chan", "sub"), None, "tile"),
    )
    out_specs = (
        P(("groups", "chan", "sub"), None, "tile"),
        P(("groups", "chan", "sub"), None, "tile"),
        P("groups", None, None),
        P("groups", None, None),
    )
    return jax.shard_map(body, mesh=mesh, in_specs=in_specs, out_specs=out_specs, check_vma=False)
```
